128 devices in a mesh: section: 8 (over y_lo, x), fsdp: 16 (over y_hi, z, core).
Axes of the slice: x: 4, y: 4 (y_hi: 2, y_lo: 2; y = y_hi * 2 + y_lo), z: 4, core: 2. Of those that a mesh axis runs over, the one named last changes fastest.
Arguments:
- section_input: bfloat16 [8, 4096, 4096], P('section', 'fsdp'), may hold values from -6 to 6
- segment_ids: int32 [8, 4096], P('section', 'fsdp'), may hold values from 0 to 2, never falling along the last dimension, each value on 1 to 3072 neighbouring positions
- query_weight: bfloat16 [8, 4096, 2048], P('section', 'fsdp'), as said below
- keyval_weight: bfloat16 [8, 4096, 512], P('section', 'fsdp'), as said below
- out_weight: bfloat16 [8, 2048, 4096], P('section', None, 'fsdp'), may hold values from -0.125 to 0.125
Outputs:
- passed: bfloat16 [8, 4096, 4096], P('section', 'fsdp')
The draws below stay inside these ranges and needn't reach their ends.
Inputs may be any that keep to these rules, and one draw needn't show every extreme that they name: `query_weight`: query projection weights. `keyval_weight`: key and value projection weights.
All inputs are finite; a program needn't handle non-finite values.
Results may differ from the reference program's by a relative error of at most 0.012.
The reference program's roundings to bfloat16 on the way count: a program that leaves them out, or rounds other values in their place, can miss the bound.
Values may be sent and summed in bfloat16 or wider, within the bound.
A program may use at most 192 MiB of HBM per device.

```python
import math
import jax
import jax.numpy as jnp
import numpy as np
from jax import lax

MODEL_WIDTH = 4096
QUERY_HEADS = 32
KEY_HEADS = 4
HEAD_SIZE = 64
LOOKBACK_SPAN = 2048
SEQUENCE_TOKENS = 4096
N_SECTION = 8


def joint_weights(key):
    base_key = jax.random.fold_in(key, 11)
    first_key, following_key = jax.random.split(base_key)
    query_raw = jnp.clip(jax.random.normal(first_key, (N_SECTION, MODEL_WIDTH, QUERY_HEADS * HEAD_SIZE), jnp.float32), -6.0, 6.0)
    unprojected_key_value = jnp.clip(jax.random.normal(following_key, (N_SECTION, MODEL_WIDTH, 2 * KEY_HEADS * HEAD_SIZE), jnp.float32), -6.0, 6.0)
    query_slice = query_raw * (2.8 / math.sqrt(MODEL_WIDTH))
    key_value_slice = unprojected_key_value * (1.0 / math.sqrt(MODEL_WIDTH))
    return (query_slice, key_value_slice)


def draw_query_weight(key, part):
    return joint_weights(key)[0].astype(jnp.bfloat16)


def draw_keyval_weight(key, part):
    return joint_weights(key)[1].astype(jnp.bfloat16)


def steps_of(own_key, shape, shards, low, largest):
    level = 1.0
    for axis_at, parts in shards:
        heights = jax.random.uniform(jax.random.fold_in(jax.random.fold_in(own_key, 6), axis_at), (parts,), jnp.float32, low / len(shards), largest / len(shards))
        level = level * jnp.repeat(jnp.exp(heights), shape[axis_at] // parts).reshape((-1,) + (1,) * (len(shape) - 1 - axis_at))
    return level


def length_profile(amount, total, reach, skew):
    portions = [(1 << 20) // math.isqrt(standing ** skew) + 1 for standing in range(2, amount + 1)]
    spare, given = total - reach - (amount - 1), [1] * (amount - 1)
    while spare > 0:
        free = [i for i in range(amount - 1) if given[i] < reach]
        pool, left = sum([portions[i] for i in free]), spare
        for i in free:
            extra = min(reach - given[i], max(1, left * portions[i] // pool), spare)
            given[i] = given[i] + extra
            spare = spare - extra
    return np.array([reach] + given)


def uneven(own_key, count, total, reach, lean):
    if count == 2:
        one = jax.random.randint(own_key, (), max(1, total - reach), min(reach, total - 1) + 1)
        return jnp.stack([one, total - one])
    tallies = jnp.asarray(length_profile(count, total, reach, lean), jnp.int32)
    couples = (count - 1) // 2
    giver, receiver = tallies[1:1 + 2 * couples:2], tallies[2:2 + 2 * couples:2]
    slack = jnp.minimum(giver - 1, reach - receiver)
    passed = jax.random.randint(jax.random.fold_in(own_key, 1), (couples,), 0, 1 << 20) % (slack + 1)
    tallies = tallies.at[1:1 + 2 * couples:2].set(giver - passed).at[2:2 + 2 * couples:2].set(receiver + passed)
    return tallies[jax.random.permutation(jax.random.fold_in(own_key, 2), count)]


def centred(key, dims, width, limit, cuts=(), held_as=jnp.bfloat16):
    drawn = width * jax.random.normal(key, dims, jnp.float32)
    if cuts:
        drawn = drawn * steps_of(key, dims, cuts, -0.22, 0.18)
    return jnp.clip(drawn, -limit, limit).astype(held_as)


def setup_inputs(seed: int = 0) -> dict:
    keys = jax.random.split(jax.random.key(seed), 6)
    return {
        "section_input": centred(keys[0], (N_SECTION, SEQUENCE_TOKENS, MODEL_WIDTH), 1.0, 6.0, ((0, 8), (1, 16))),
        "segment_ids": jax.vmap(lambda own: jnp.searchsorted(jnp.cumsum(uneven(own, 3, SEQUENCE_TOKENS, 3 * SEQUENCE_TOKENS // 4, 0)), jnp.arange(SEQUENCE_TOKENS), side="right"))(jax.random.split(keys[1], N_SECTION)).reshape((N_SECTION, SEQUENCE_TOKENS)).astype(jnp.int32),
        "query_weight": draw_query_weight(jax.random.fold_in(keys[5], 71), 0),
        "keyval_weight": draw_keyval_weight(jax.random.fold_in(keys[5], 71), 0),
        "out_weight": centred(keys[4], (N_SECTION, QUERY_HEADS * HEAD_SIZE, MODEL_WIDTH), (QUERY_HEADS * HEAD_SIZE) ** -0.5, 0.125, ((0, 8), (2, 16))),
    }


def normed(values):
    widened = values.astype(jnp.float32)
    scaled = widened * lax.rsqrt(lax.optimization_barrier(jnp.mean(widened * widened, axis=-1, keepdims=True)) + 1e-05)
    return scaled.astype(jnp.bfloat16)

def apply_layer(hidden, segments, query_weight, keyval_weight, out_weight):
    queries_per_group = QUERY_HEADS // KEY_HEADS
    normal_rows = normed(hidden)
    query_rows = jnp.dot(normal_rows, query_weight, preferred_element_type=jnp.float32).astype(jnp.bfloat16)
    key_value_rows = jnp.dot(normal_rows, keyval_weight, preferred_element_type=jnp.float32).astype(jnp.bfloat16)
    key_lines = key_value_rows[:, :KEY_HEADS * HEAD_SIZE].reshape(SEQUENCE_TOKENS, KEY_HEADS, HEAD_SIZE)
    value_lines = key_value_rows[:, KEY_HEADS * HEAD_SIZE:].reshape(SEQUENCE_TOKENS, KEY_HEADS, HEAD_SIZE)
    padded_keys = jnp.concatenate([jnp.zeros((LOOKBACK_SPAN, KEY_HEADS, HEAD_SIZE), jnp.bfloat16), key_lines], axis=0)
    padded_values = jnp.concatenate([jnp.zeros((LOOKBACK_SPAN, KEY_HEADS, HEAD_SIZE), jnp.bfloat16), value_lines], axis=0)
    seg_int = segments.astype(jnp.int32)
    seg_padded = jnp.concatenate([jnp.full((LOOKBACK_SPAN,), -1, jnp.int32), seg_int], axis=0)
    rows_per_block = math.gcd(SEQUENCE_TOKENS, 512)
    key_span = LOOKBACK_SPAN + rows_per_block

    def attend(block_index):
        first_row = (block_index * rows_per_block).astype(jnp.int32)
        query_tile = lax.dynamic_slice_in_dim(query_rows, first_row, rows_per_block, 0)
        query_tile = query_tile.reshape(rows_per_block, KEY_HEADS, queries_per_group, HEAD_SIZE).astype(jnp.float32)
        key_block = lax.dynamic_slice_in_dim(padded_keys, first_row, key_span, 0).astype(jnp.float32)
        value_block = lax.dynamic_slice_in_dim(padded_values, first_row, key_span, 0).astype(jnp.float32)
        key_segs = lax.dynamic_slice_in_dim(seg_padded, first_row, key_span, 0)
        query_segs = lax.dynamic_slice_in_dim(seg_int, first_row, rows_per_block, 0)
        query_pos = first_row + jnp.arange(rows_per_block, dtype=jnp.int32)
        key_pos = first_row - LOOKBACK_SPAN + jnp.arange(key_span, dtype=jnp.int32)
        scores = jnp.einsum('qhgd,khd->hgqk', query_tile, key_block) * HEAD_SIZE ** (-0.5)
        visible = (query_segs[:, None] == key_segs[None, :]) & (key_pos[None, :] <= query_pos[:, None])
        visible = visible & (key_pos[None, :] > query_pos[:, None] - LOOKBACK_SPAN) & (key_pos[None, :] >= 0)
        scores = jnp.where(visible, scores, -1e+30)
        row_peak = lax.optimization_barrier(jnp.max(scores, axis=-1, keepdims=True))
        weights = jnp.where(visible, jnp.exp(scores - row_peak), 0.0)
        weight_sum = lax.optimization_barrier(jnp.sum(weights, axis=-1))
        rounded = lax.optimization_barrier(weights.astype(jnp.bfloat16)).astype(jnp.float32)
        mixed_heads = jnp.einsum('hgqk,khd->hgqd', rounded, value_block) / weight_sum[..., None]
        return jnp.transpose(mixed_heads, (2, 0, 1, 3)).reshape(rows_per_block, QUERY_HEADS * HEAD_SIZE).astype(jnp.bfloat16)
    attended = lax.map(attend, jnp.arange(SEQUENCE_TOKENS // rows_per_block, dtype=jnp.int32)).reshape(SEQUENCE_TOKENS, QUERY_HEADS * HEAD_SIZE)
    projected = jnp.dot(attended, out_weight, preferred_element_type=jnp.float32)
    return (hidden.astype(jnp.float32) + projected).astype(jnp.bfloat16)

def reference(section_input, segment_ids, query_weight, keyval_weight, out_weight):
    results = []
    for section_index in range(N_SECTION):
        results.append(apply_layer(section_input[section_index], segment_ids[section_index], query_weight[section_index], keyval_weight[section_index], out_weight[section_index]))
    stacked = jnp.stack(results)
    return jnp.roll(stacked, 1, axis=0)
```

```python
import jax
import jax.numpy as jnp
from jax import lax
from jax.experimental import pallas as pl
from jax.experimental.pallas import tpu as pltpu
from jax.sharding import Mesh, PartitionSpec as P

BF = jnp.bfloat16
F32 = jnp.float32
MESH = pl.DeviceIdType.MESH

KV, Q0, Q1, Q2, Q3, KX, O0, O1 = range(8)


def kernel(hid, segrow, segcol, wq, wkv, wo, out,
           x, wb, wob, kvb, qs, att, hf, outb, sbuf, acc, qst, sgr, sgc, lod,
           ss, rs, ls, ns, nr, ws, wr, hs, hr, hl, gs, gr, xs, xr, a_s, a_r, ps, pr):
    sec, yh, z, c = (lax.axis_index(n) for n in ("section", "yh", "z", "core"))
    oc = 1 - c
    b = yh * 4 + z
    zp, zm, zz = (z + 1) % 4, (z + 3) % 4, (z + 2) % 4
    oy = 1 - yh
    SIB = (sec, yh, z, oc)
    YP = (sec, oy, z, c)
    ZP = (sec, yh, zp, c)
    ZM = (sec, yh, zm, c)
    nxt, prv = (sec + 1) % 8, (sec + 7) % 8
    NX = [(nxt, yh, z, 0), (nxt, yh, z, 1)]
    PV = [(prv, yh, z, 0), (prv, yh, z, 1)]

    def rcopy(src, dst, send, recv, dev):
        return pltpu.make_async_remote_copy(
            src_ref=src, dst_ref=dst, send_sem=send, recv_sem=recv,
            device_id=dev, device_id_type=MESH)

    bar = pltpu.get_barrier_semaphore()
    for d in [SIB, YP, ZP, ZM] + NX + PV:
        pl.semaphore_signal(bar, inc=1, device_id=d, device_id_type=MESH)
    pl.semaphore_wait(bar, 8)

    def rows256(k):
        return pl.ds(pl.multiple_of(256 * k, 256), 256)

    def blk(ci, owner):
        if ci <= Q3:
            return wb.at[ci, owner]
        if ci == KX:
            return kvb.at[owner]
        return wob.at[ci - O0, owner]

    def half(ci, owner, h):
        n = 256 if ci <= Q3 else (272 if ci == KX else 1024)
        return blk(ci, owner).at[pl.ds(n * h, n)]

    OWN, PAR = b, oy * 4 + z
    own = lambda dy, dz: ((yh + dy) % 2) * 4 + (z + dz) % 4

    def sendc(ci, i):
        src, dev = {
            0: lambda: (blk(ci, OWN), YP),
            1: lambda: (blk(ci, OWN), ZP),
            2: lambda: (blk(ci, OWN), ZM),
            3: lambda: (blk(ci, PAR), ZP),
            4: lambda: (blk(ci, PAR), ZM),
            5: lambda: (half(ci, own(0, 3), 0), ZP),
            6: lambda: (half(ci, own(0, 1), 1), ZM),
            7: lambda: (blk(ci, own(0, 2)), YP),
        }[i]()
        return rcopy(src, src, ss.at[ci, i], rs.at[ci, i], dev)

    def waitc(ci, i):
        dst = {
            0: lambda: blk(ci, PAR),
            1: lambda: blk(ci, own(0, 3)),
            2: lambda: blk(ci, own(0, 1)),
            3: lambda: blk(ci, own(1, 3)),
            4: lambda: blk(ci, own(1, 1)),
            5: lambda: half(ci, own(0, 2), 0),
            6: lambda: half(ci, own(0, 2), 1),
            7: lambda: blk(ci, own(1, 2)),
        }[i]()
        rcopy(dst, dst, ss.at[ci, i], rs.at[ci, i], YP).wait_recv()

    def own_pieces(ci):
        if ci == KV:
            return [(wkv, 128 * c, 128 * oc, 0, 128), (wkv, 256 + 128 * c, 256 + 128 * oc, 128, 128)]
        k = ci - Q0
        return [(wq, 1024 * c + 256 * k, 1024 * oc + 256 * k, 0, 256)]

    def fill_copies(ci):
        loc, rem = [], []
        for n, (w, mine, theirs, lane, width) in enumerate(own_pieces(ci)):
            dst = wb.at[ci, b, rows256(c), pl.ds(lane, width)]
            loc.append(pltpu.make_async_copy(
                w.at[:, pl.ds(pl.multiple_of(mine, 128), width)], dst, ls.at[ci, n]))
            rem.append(rcopy(
                w.at[:, pl.ds(pl.multiple_of(theirs, 128), width)], dst,
                ws.at[ci, n], wr.at[ci, n], SIB))
        return loc, rem

    def fill_waits(ci):
        for n, (w, mine, theirs, lane, width) in enumerate(own_pieces(ci)):
            dst = wb.at[ci, b, rows256(c), pl.ds(lane, width)]
            pltpu.make_async_copy(
                w.at[:, pl.ds(pl.multiple_of(mine, 128), width)], dst, ls.at[ci, n]).wait()
        for n, (w, mine, theirs, lane, width) in enumerate(own_pieces(ci)):
            dst = wb.at[ci, b, rows256(oc), pl.ds(lane, width)]
            rcopy(dst, dst, ws.at[ci, n], wr.at[ci, n], SIB).wait_recv()

    def wo_fill(h):
        return pltpu.make_async_copy(wo.at[:, pl.ds(128 * h, 128)], wob.at[h, b], ls.at[O0 + h, 0])

    for ci in (KV, Q0, Q1, Q2, Q3):
        loc, rem = fill_copies(ci)
        for d in rem + loc:
            d.start()
    for h in (0, 1):
        wo_fill(h).start()

    g1 = rcopy(sgr.at[c], sgr.at[c], gs.at[0], gr.at[0], SIB)
    g2 = rcopy(sgc.at[c], sgc.at[c], gs.at[1], gr.at[1], SIB)
    sgr[c] = segrow[...]
    sgc[c] = segcol[...]
    g1.start()
    g2.start()

    def hid_cols(o, cc):
        return hid.at[:, pl.ds(pl.multiple_of(256 * (2 * o + cc), 256), 256)]

    def hid_remote(o):
        return rcopy(hid_cols(o, oc), hf.at[c, o], hs.at[o], hr.at[o], SIB)

    def hid_local(o):
        return pltpu.make_async_copy(hid_cols(o, c), hf.at[c, o], hl.at[o])

    def phase_a(ci):
        if ci <= Q3:
            fill_waits(ci)
        elif ci >= O0:
            wo_fill(ci - O0).wait()
        for i in (0, 1, 2):
            sendc(ci, i).start()

    def phase_b(ci):
        waitc(ci, 0)
        sendc(ci, 3).start()
        sendc(ci, 4).start()
        waitc(ci, 1)
        sendc(ci, 5).start()
        waitc(ci, 2)
        sendc(ci, 6).start()

    def phase_c(ci):
        waitc(ci, 5)
        waitc(ci, 6)
        sendc(ci, 7).start()
        waitc(ci, 3)
        waitc(ci, 4)

    def phase_d(ci):
        waitc(ci, 7)

    def gemm(ci):
        acc[...] = jnp.zeros_like(acc)

        def step(o, carry):
            acc[...] += jnp.dot(x[o], wb[ci, o], preferred_element_type=F32)
            return carry

        lax.fori_loop(0, 8, step, 0)

    phase_a(KV)
    phase_a(Q0)

    def norm(i, carry):
        r = pl.ds(pl.multiple_of(32 * i, 32), 32)
        v = hid[r, :].astype(F32)
        v = v * lax.rsqrt(jnp.mean(v * v, axis=-1, keepdims=True) + 1e-05)
        v = v.astype(BF)
        dst = pl.ds(pl.multiple_of(256 * c + 32 * i, 32), 32)
        for o in range(8):
            x[o, dst, :] = v[:, 512 * o:512 * o + 512]
        return carry

    lax.fori_loop(0, 8, norm, 0)
    xc = rcopy(x.at[:, rows256(c)], x.at[:, rows256(c)], ns, nr, SIB)
    xc.start()
    for o in range(8):
        hid_remote(o).start()
        hid_local(o).start()

    phase_b(KV)
    phase_a(Q1)
    phase_c(KV)
    phase_b(Q0)
    xw = x.at[:, rows256(oc)]
    rcopy(xw, xw, ns, nr, SIB).wait_recv()
    phase_d(KV)
    gemm(KV)
    kvb[b, 0:512, :] = acc[...].astype(BF)
    for i in (0, 1):
        w_ = (sgr.at[oc], sgc.at[oc])[i]
        rcopy(w_, w_, gs.at[i], gr.at[i], SIB).wait_recv()
    kvb[b, 512:528, :] = sgr[0]
    kvb[b, 528:544, :] = sgr[1]
    phase_a(KX)

    def put_q(k):
        gemm(Q0 + k)
        qs[2 * k] = acc[:, 0:128].astype(BF)
        qs[2 * k + 1] = acc[:, 128:256].astype(BF)

    phase_c(Q0)
    phase_b(KX)
    phase_a(Q2)
    phase_b(Q1)
    phase_d(Q0)
    put_q(0)
    phase_c(KX)
    phase_c(Q1)
    phase_a(Q3)
    phase_b(Q2)
    phase_d(KX)

    lane = lax.broadcasted_iota(jnp.int32, (256, 128), 1)
    row = lax.broadcasted_iota(jnp.int32, (256, 128), 0)
    below1 = jnp.zeros((16, 256), F32)
    below2 = jnp.zeros((16, 256), F32)
    for o in range(8):
        for t in (512, 528):
            g = kvb[o, t:t + 16, :].astype(F32)
            below1 = below1 + jnp.where(g < 0.5, 1.0, 0.0)
            below2 = below2 + jnp.where(g < 1.5, 1.0, 0.0)
    n1 = jnp.sum(below1[0:8], axis=-1, keepdims=True)[0:1, :]
    n2 = jnp.sum(below2[0:8], axis=-1, keepdims=True)[0:1, :]
    for j in (0, 1):
        g = sgc[j].astype(F32)
        start = jnp.where(g < 0.5, 0.0, jnp.where(g < 1.5, n1, n2)).astype(jnp.int32)
        pos = 512 * b + 256 * j + row
        lod[j] = jnp.maximum(start, pos - 2047) - lane

    low = lane < 64

    def attend(k):
        first_head = k < 2

        def one(it, carry):
            p = 2 * k + it // 2
            j = it % 2
            jr = rows256(j)
            q2 = qs[p, jr, :].astype(F32)
            qr = pltpu.roll(q2, 64, 1)
            zero = jnp.zeros_like(q2)
            if first_head:
                qe, qo = jnp.where(low, q2, zero), jnp.where(low, qr, zero)
            else:
                qe, qo = jnp.where(low, zero, qr), jnp.where(low, zero, q2)
            qst[0:256, :] = qe.astype(BF)
            qst[256:512, :] = qo.astype(BF)
            d1 = lod[j]
            m = jnp.full((512, 128), -1e30, F32)
            for t in range(9):
                kb = (2 * b + j + t + 8) % 16
                kk = kvb[kb // 2, rows256(kb % 2), 0:128]
                s = lax.dot_general(qst[...], kk, (((1,), (1,)), ((), ())),
                                    preferred_element_type=F32)
                base = 256 * (2 * b + j + t) - 2048
                for u in (0, 1):
                    ok = d1 <= base + 128 * u
                    if t == 8:
                        ok = ok & (row - lane >= 128 * u)
                    ok = jnp.concatenate([ok, ok], axis=0)
                    su = jnp.where(ok, s[:, 128 * u:128 * u + 128], -1e30)
                    sbuf[t, :, 128 * u:128 * u + 128] = su
                    m = jnp.maximum(m, su)
            mm = jnp.max(m, axis=-1, keepdims=True)
            l = jnp.zeros((512, 128), F32)
            o_ = jnp.zeros((512, 128), F32)
            for t in range(9):
                kb = (2 * b + j + t + 8) % 16
                vv = kvb[kb // 2, rows256(kb % 2), 128:256]
                w = jnp.exp((sbuf[t] - mm) * 0.125)
                l = l + w[:, 0:128] + w[:, 128:256]
                o_ = o_ + jnp.dot(w.astype(BF), vv, preferred_element_type=F32)
            o_ = o_ / jnp.sum(l, axis=-1, keepdims=True)
            oe, oo = o_[0:256], o_[256:512]
            if first_head:
                res = jnp.where(low, oe, pltpu.roll(oo, 64, 1))
            else:
                res = jnp.where(low, pltpu.roll(oe, 64, 1), oo)
            att[jr, pl.ds(pl.multiple_of(1024 * c + 128 * p, 128), 128)] = res.astype(BF)
            return carry

        lax.fori_loop(0, 4, one, 0)
        cols = pl.ds(pl.multiple_of(1024 * c + 256 * k, 256), 256)
        rcopy(att.at[:, cols], att.at[:, cols], a_s.at[k], a_r.at[k], SIB).start()

    attend(0)
    phase_d(Q1)
    put_q(1)
    phase_a(O0)
    phase_c(Q2)
    phase_b(Q3)
    attend(1)
    phase_d(Q2)
    put_q(2)
    phase_a(O1)
    phase_c(Q3)
    phase_b(O0)
    attend(2)
    phase_d(Q3)
    put_q(3)
    phase_c(O0)
    phase_b(O1)
    attend(3)

    for k in range(4):
        cols = pl.ds(pl.multiple_of(1024 * oc + 256 * k, 256), 256)
        w_ = att.at[:, cols]
        rcopy(w_, w_, a_s.at[k], a_r.at[k], SIB).wait_recv()
    for o in range(8):
        hid_local(o).wait()
        w_ = hf.at[oc, o]
        rcopy(w_, w_, hs.at[o], hr.at[o], SIB).wait_recv()

    def out_cols(o, cc, h):
        return out.at[:, pl.ds(pl.multiple_of(256 * (2 * o + cc) + 128 * h, 128), 128)]

    def pass_copy(h, o, cc):
        return rcopy(outb.at[h, o, cc], out_cols(o, c, h), ps.at[h, o, cc], pr.at[h, o, c], NX[cc])

    def project(h, n, dy, dz):
        def step(i, carry):
            o = own(dy(i), dz(i))
            v = jnp.dot(att[...], wob[h, o], preferred_element_type=F32)
            for cc in (0, 1):
                r = v[256 * cc:256 * cc + 256] + hf[cc, o, :, 128 * h:128 * h + 128].astype(F32)
                outb[h, o, cc] = r.astype(BF)
                pass_copy(h, o, cc).start()
            return carry

        lax.fori_loop(0, n, step, 0)

    def project_b(h):
        project(h, 2, lambda i: i, lambda i: 0)
        project(h, 2, lambda i: 0, lambda i: 1 + 2 * i)

    def project_c(h):
        project(h, 2, lambda i: 1, lambda i: 1 + 2 * i)
        project(h, 1, lambda i: 0, lambda i: 2)

    def project_d(h):
        project(h, 1, lambda i: 1, lambda i: 2)

    project_b(0)
    project_c(0)
    phase_d(O0)
    project_d(0)
    project_b(1)
    phase_c(O1)
    project_c(1)
    phase_d(O1)
    project_d(1)

    for ci in range(8):
        for i in range(8):
            sendc(ci, i).wait_send()
    for ci in (KV, Q0, Q1, Q2, Q3):
        for d in fill_copies(ci)[1]:
            d.wait_send()
    g1.wait_send()
    g2.wait_send()
    xc.wait_send()
    for o in range(8):
        hid_remote(o).wait_send()
    for k in range(4):
        cols = pl.ds(pl.multiple_of(1024 * c + 256 * k, 256), 256)
        rcopy(att.at[:, cols], att.at[:, cols], a_s.at[k], a_r.at[k], SIB).wait_send()
    for h in (0, 1):
        for o in range(8):
            for cc in (0, 1):
                pass_copy(h, o, cc).wait_send()
                w_ = out_cols(o, cc, h)
                rcopy(w_, w_, ps.at[h, o, cc], pr.at[h, o, cc], NX[cc]).wait_recv()


def body(section_input, segment_ids, query_weight, keyval_weight, out_weight):
    hidden = section_input[0]
    seg = segment_ids[0].astype(BF)
    segrow = jnp.broadcast_to(seg[None, :], (16, 256))
    segcol = jnp.broadcast_to(seg[:, None], (256, 128))
    vm = pl.BlockSpec(memory_space=pltpu.VMEM)
    hb = pl.BlockSpec(memory_space=pl.ANY)
    dma = pltpu.SemaphoreType.DMA
    res = pl.pallas_call(
        kernel,
        out_shape=jax.ShapeDtypeStruct((256, 4096), BF),
        in_specs=[vm, vm, vm, hb, hb, hb],
        out_specs=hb,
        scratch_shapes=[
            pltpu.VMEM((8, 512, 512), BF),
            pltpu.VMEM((5, 8, 512, 256), BF),
            pltpu.VMEM((2, 8, 2048, 128), BF),
            pltpu.VMEM((8, 544, 256), BF),
            pltpu.VMEM((8, 512, 128), BF),
            pltpu.VMEM((512, 2048), BF),
            pltpu.VMEM((2, 8, 256, 256), BF),
            pltpu.VMEM((2, 8, 2, 256, 128), BF),
            pltpu.VMEM((9, 512, 256), F32),
            pltpu.VMEM((512, 256), F32),
            pltpu.VMEM((512, 128), BF),
            pltpu.VMEM((2, 16, 256), BF),
            pltpu.VMEM((2, 256, 128), BF),
            pltpu.VMEM((2, 256, 128), jnp.int32),
            dma((8, 8)), dma((8, 8)),
            dma((8, 2)),
            dma, dma,
            dma((5, 2)), dma((5, 2)),
            dma((8,)), dma((8,)), dma((8,)),
            dma((2,)), dma((2,)),
            dma, dma,
            dma((4,)), dma((4,)),
            dma((2, 8, 2)), dma((2, 8, 2)),
        ],
        compiler_params=pltpu.CompilerParams(
            collective_id=0, has_side_effects=True, vmem_limit_bytes=58 << 20),
        name="layer",
    )(hidden, segrow, segcol, query_weight[0], keyval_weight[0], out_weight[0])
    return res[None]


def solution(mesh):
    fine = Mesh(mesh.devices.reshape(8, 2, 4, 2), ("section", "yh", "z", "core"))
    tok = ("yh", "z", "core")
    return jax.shard_map(
        body,
        mesh=fine,
        in_specs=(
            P("section", tok, None),
            P("section", tok),
            P("section", tok, None),
            P("section", tok, None),
            P("section", None, tok),
        ),
        out_specs=P("section", tok, None),
        check_vma=False,
    )
```

```python
import jax
import jax.numpy as jnp
from jax import lax
from jax.experimental import pallas as pl
from jax.experimental.pallas import tpu as pltpu
from jax.sharding import Mesh, PartitionSpec as P

BF = jnp.bfloat16
F32 = jnp.float32
MESH = pl.DeviceIdType.MESH
EXP_SCALE = 0.125 * 1.4426950408889634

KV, QA, QB, KX = range(4)


def kernel(hid, seg, wq, wkv, wo, out,
           x, wqb, wkvb, wob, kvb, qs, att, atx, hf, outb, accq, acck, ostat, sgr, lod,
           fs, fr, fl, zs, zr, os_, or_, ol, xs, xr, hs, hr, hl, gs, gr, axs, axr, ps, pr, rly, rs, rr):
    sec, yh, z, c = (lax.axis_index(n) for n in ("section", "yh", "z", "core"))
    oc, oy = 1 - c, 1 - yh
    u = 2 * yh + c
    u_sib, u_y, u_yx = 2 * yh + oc, 2 * oy + c, 2 * oy + oc
    b = yh * 4 + z
    zp, zm = (z + 1) % 4, (z + 3) % 4
    SIB = (sec, yh, z, oc)
    YP = (sec, oy, z, c)
    YX = (sec, oy, z, oc)
    ZP = (sec, yh, zp, c)
    ZM = (sec, yh, zm, c)
    nxt, prv = (sec + 1) % 8, (sec + 7) % 8
    NX = [(nxt, yh, z, 0), (nxt, yh, z, 1)]
    PV = [(prv, yh, z, 0), (prv, yh, z, 1)]
    wrap = sec % 4 == 3
    MID = ((sec + 4) % 8, yh, z, c)
    FAR = [((sec + 5) % 8, yh, z, k) for k in (0, 1)]
    NEAR = [((sec + 3) % 8, yh, z, k) for k in (0, 1)]

    def rcopy(src, dst, send, recv, dev):
        return pltpu.make_async_remote_copy(
            src_ref=src, dst_ref=dst, send_sem=send, recv_sem=recv,
            device_id=dev, device_id_type=MESH)

    def got(dst, send, recv):
        rcopy(dst, dst, send, recv, SIB).wait_recv()

    def al(v, n):
        return pl.multiple_of(v, n)

    def r256(k):
        return pl.ds(al(256 * k, 256), 256)

    bar = pltpu.get_barrier_semaphore()
    for d in [SIB, YP, YX, ZP, ZM, MID] + NX + PV + FAR + NEAR:
        pl.semaphore_signal(bar, inc=1, device_id=d, device_id_type=MESH)
    pl.semaphore_wait(bar, 14)

    def quarter(ci, v):
        if ci == KV:
            return wkv.at[:, pl.ds(al(128 * v, 128), 128)]
        return wq.at[:, pl.ds(al(512 * v + 256 * (ci - QA), 256), 256)]

    def rb(ci, zo):
        if ci == KV:
            return wkvb.at[zo]
        if ci == KX:
            return kvb.at[zo]
        return wqb.at[ci - QA, zo]

    def fill(ci, n):
        v, dev = [(u_y, YP), (u_yx, YX), (u_sib, SIB)][n]
        return rcopy(quarter(ci, v), rb(ci, z).at[r256(u)], fs.at[ci, n], fr.at[ci, u], dev)

    def fill_local(ci):
        return pltpu.make_async_copy(quarter(ci, u), rb(ci, z).at[r256(u)], fl.at[ci])

    def fill_wait(ci):
        fill_local(ci).wait()
        for v in (u_sib, u_y, u_yx):
            got(rb(ci, z).at[r256(v)], fs.at[ci, 0], fr.at[ci, v])

    def rhalf(ci, zo, h):
        n = 576 if ci == KX else 512
        return rb(ci, zo).at[pl.ds(n * h, n)]

    def ring(ci, i):
        src, dev = {
            0: lambda: (rb(ci, z), ZP),
            1: lambda: (rb(ci, z), ZM),
            2: lambda: (rhalf(ci, zm, 0), ZP),
            3: lambda: (rhalf(ci, zp, 1), ZM),
        }[i]()
        return rcopy(src, src, zs.at[ci, i], zr.at[ci, i], dev)

    def ring_got(ci, i):
        dst = {
            0: lambda: rb(ci, zm),
            1: lambda: rb(ci, zp),
            2: lambda: rhalf(ci, (z + 2) % 4, 0),
            3: lambda: rhalf(ci, (z + 2) % 4, 1),
        }[i]()
        got(dst, zs.at[ci, i], zr.at[ci, i])

    def ring_a(ci):
        ring(ci, 0).start()
        ring(ci, 1).start()

    def ring_b(ci):
        ring_got(ci, 0)
        ring(ci, 2).start()
        ring_got(ci, 1)
        ring(ci, 3).start()

    def ring_c(ci):
        ring_got(ci, 2)
        ring_got(ci, 3)

    def own(dy, dz):
        return ((yh + dy) % 2) * 4 + (z + dz) % 4

    def ob(h, dy, dz):
        return wob.at[h, own(dy, dz)]

    def oh(h, dy, dz, k):
        return wob.at[h, own(dy, dz), pl.ds(1024 * k, 1024)]

    def osend(h, i):
        src, dev = {
            0: lambda: (ob(h, 0, 0), YP),
            1: lambda: (ob(h, 0, 0), ZP),
            2: lambda: (ob(h, 0, 0), ZM),
            3: lambda: (ob(h, 1, 0), ZP),
            4: lambda: (ob(h, 1, 0), ZM),
            5: lambda: (oh(h, 0, 3, 0), ZP),
            6: lambda: (oh(h, 0, 1, 1), ZM),
            7: lambda: (ob(h, 0, 2), YP),
        }[i]()
        return rcopy(src, src, os_.at[h, i], or_.at[h, i], dev)

    def ogot(h, i):
        dst = {
            0: lambda: ob(h, 1, 0),
            1: lambda: ob(h, 0, 3),
            2: lambda: ob(h, 0, 1),
            3: lambda: ob(h, 1, 3),
            4: lambda: ob(h, 1, 1),
            5: lambda: oh(h, 0, 2, 0),
            6: lambda: oh(h, 0, 2, 1),
            7: lambda: ob(h, 1, 2),
        }[i]()
        got(dst, os_.at[h, i], or_.at[h, i])

    def o_fill(h):
        return pltpu.make_async_copy(wo.at[:, pl.ds(128 * h, 128)], wob.at[h, b], ol.at[h])

    def o_az(h):
        o_fill(h).wait()
        osend(h, 1).start()
        osend(h, 2).start()

    def o_ay(h):
        osend(h, 0).start()

    def o_b1(h):
        ogot(h, 1)
        osend(h, 5).start()
        ogot(h, 2)
        osend(h, 6).start()

    def o_b2(h):
        ogot(h, 0)
        osend(h, 3).start()
        osend(h, 4).start()

    def o_zz(h):
        ogot(h, 5)
        ogot(h, 6)
        osend(h, 7).start()

    def o_c(h):
        ogot(h, 3)
        ogot(h, 4)

    def o_d(h):
        ogot(h, 7)

    for ci in (KV, QA, QB):
        for n in range(3):
            fill(ci, n).start()
        fill_local(ci).start()
    for h in (0, 1):
        o_fill(h).start()

    def segs(n):
        return rcopy(sgr.at[u], sgr.at[u], gs.at[n], gr.at[u], [YP, YX, SIB][n])

    sgr[u] = seg[...]
    for n in range(3):
        segs(n).start()

    def hid_cols(o, cc):
        return hid.at[:, pl.ds(al(256 * (2 * o + cc), 256), 256)]

    def hid_remote(o):
        return rcopy(hid_cols(o, oc), hf.at[c, o], hs.at[o], hr.at[o], SIB)

    def hid_local(o):
        return pltpu.make_async_copy(hid_cols(o, c), hf.at[c, o], hl.at[o])

    def norm(i, carry):
        r = pl.ds(al(32 * i, 32), 32)
        v = hid[r, :].astype(F32)
        v = v * lax.rsqrt(jnp.mean(v * v, axis=-1, keepdims=True) + 1e-05)
        v = v.astype(BF)
        dst = pl.ds(al(256 * u + 32 * i, 32), 32)
        for d in range(16):
            lanes = 256 * (2 * (d // 8) + d % 2)
            x[(d // 2) % 4, dst, lanes:lanes + 256] = v[:, 256 * d:256 * d + 256]
        return carry

    lax.fori_loop(0, 8, norm, 0)

    def xcopy(k, q):
        v, dev = [(u, YP), (u, SIB), (u_y, SIB)][k]
        ref = x.at[q, r256(v)]
        return rcopy(ref, ref, xs.at[k, q], xr.at[k, q], dev)

    def xgot(k, q):
        v = [u_y, u_sib, u_yx][k]
        got(x.at[q, r256(v)], xs.at[k, q], xr.at[k, q])

    for q in range(4):
        xcopy(0, q).start()
        xcopy(1, q).start()

    def x_forward(q):
        xgot(0, q)
        xcopy(2, q).start()

    acck[...] = jnp.zeros_like(acck)
    accq[...] = jnp.zeros_like(accq)

    def gemm(yr, lo, hi):
        rows = pl.ds(al(512 * yr, 512), 512)

        def step(q, carry):
            xv = x[q, rows, :]
            acck[rows, :] += jnp.dot(xv, wkvb[q], preferred_element_type=F32)
            for k in (0, 1):
                accq[k, rows, :] += jnp.dot(xv, wqb[k, q], preferred_element_type=F32)
            return carry

        lax.fori_loop(lo, hi, step, 0)

    for ci in (KV, QA, QB):
        fill_wait(ci)
        ring_a(ci)
    for o in range(8):
        hid_remote(o).start()
        hid_local(o).start()
    ring_b(KV)
    x_forward(0)
    ring_b(QA)
    for q in range(4):
        xgot(1, q)
    x_forward(1)
    ring_b(QB)
    o_az(0)
    ring_c(KV)
    ring_c(QA)
    x_forward(2)
    ring_c(QB)
    o_az(1)
    gemm(yh, 0, 4)
    xgot(2, 0)
    xgot(2, 1)
    gemm(oy, 0, 2)
    xgot(2, 2)
    gemm(oy, 2, 3)
    x_forward(3)
    o_ay(0)
    o_ay(1)
    xgot(2, 3)
    gemm(oy, 3, 4)
    kvb[z, 0:1024, :] = acck[...].astype(BF)
    for v in (u_sib, u_y, u_yx):
        got(sgr.at[v], gs.at[0], gr.at[v])
    for k in range(4):
        kvb[z, 1024 + 32 * k:1056 + 32 * k, :] = sgr[k]
    ring_a(KX)
    for p in range(4):
        qs[p] = accq[p // 2, :, 128 * (p % 2):128 * (p % 2) + 128].astype(BF)
    o_b1(0)
    ring_b(KX)
    o_b1(1)
    ring_c(KX)
    o_b2(0)

    lane = lax.broadcasted_iota(jnp.int32, (256, 128), 1)
    row = lax.broadcasted_iota(jnp.int32, (256, 128), 0)
    low = lane < 64
    below1 = jnp.zeros((16, 128), F32)
    below2 = jnp.zeros((16, 128), F32)
    for q in range(4):
        for t in range(1024, 1152, 16):
            g = kvb[q, t:t + 16, :].astype(F32)
            below1 = below1 + jnp.where(g < 0.5, 1.0, 0.0)
            below2 = below2 + jnp.where(g < 1.5, 1.0, 0.0)
    n1 = jnp.sum(below1[0:8], axis=-1, keepdims=True)[0:1, :]
    n2 = jnp.sum(below2[0:8], axis=-1, keepdims=True)[0:1, :]
    for r in range(4):
        g = jnp.concatenate(
            [jnp.transpose(jnp.broadcast_to(sgr[r, 16 * k:16 * k + 16, :].astype(F32)[0:1, :], (128, 128)))
             for k in (0, 1)], axis=0)
        start = jnp.where(g < 0.5, 0.0, jnp.where(g < 1.5, n1, n2)).astype(jnp.int32)
        pos = 2048 * (r // 2) + 512 * z + 256 * (r % 2) + row
        lod[r] = jnp.maximum(start, pos - 2047) - lane

    def attend(yr, cr, mine):
        r = 2 * yr + cr
        rblk = 2 * (4 * yr + z) + cr

        def one(p, carry):
            q2 = qs[p, r256(r), :].astype(F32)
            zero = jnp.zeros_like(q2)
            d1 = lod[r]
            for hh in (0, 1):
                q1 = jnp.where(low, q2 if hh == 0 else pltpu.roll(q2, 64, 1), zero).astype(BF)
                ss = []
                m = jnp.full((256, 128), -1e30, F32)
                for t in range(9):
                    kb = (rblk + t + 8) % 16
                    kk = kvb[(kb // 2) % 4, r256(2 * (kb // 8) + kb % 2), :]
                    s = lax.dot_general(q1, kk, (((1,), (1,)), ((), ())),
                                        preferred_element_type=F32)
                    base = 256 * (rblk + t) - 2048
                    for v in (0, 1):
                        ok = d1 <= base + 128 * v
                        if t == 8:
                            ok = ok & (row - lane >= 128 * v)
                        su = jnp.where(ok, s[:, 128 * v:128 * v + 128], -1e30)
                        ss.append(su)
                        m = jnp.maximum(m, su)
                mm = jnp.max(m, axis=-1, keepdims=True)
                l = jnp.zeros((256, 128), F32)
                o_ = jnp.zeros((256, 128), F32)
                for t in range(9):
                    kb = (rblk + t + 8) % 16
                    kk = kvb[(kb // 2) % 4, r256(2 * (kb // 8) + kb % 2), :]
                    w0 = jnp.exp2((ss[2 * t] - mm) * EXP_SCALE)
                    w1 = jnp.exp2((ss[2 * t + 1] - mm) * EXP_SCALE)
                    l = l + w0 + w1
                    o_ = o_ + jnp.dot(jnp.concatenate([w0, w1], axis=1).astype(BF), kk,
                                      preferred_element_type=F32)
                ostat[hh] = o_ / jnp.sum(l, axis=-1, keepdims=True)
            res = jnp.where(low, pltpu.roll(ostat[0], 64, 1), ostat[1]).astype(BF)
            if mine:
                att[r256(cr), pl.ds(al(512 * u + 128 * p, 128), 128)] = res
            else:
                atx[cr, :, pl.ds(al(128 * p, 128), 128)] = res
            return carry

        lax.fori_loop(0, 4, one, 0, unroll=2)

    def ablk(cr, v):
        return att.at[r256(cr), pl.ds(al(512 * v, 512), 512)]

    def acopy(k, cr):
        src, dst, dev = [
            lambda: (atx.at[cr], ablk(cr, u), YP),
            lambda: (ablk(cr, u), ablk(cr, u), SIB),
            lambda: (ablk(cr, u_y), ablk(cr, u_y), SIB),
        ][k]()
        return rcopy(src, dst, axs.at[k, cr], axr.at[k, cr], dev)

    def agot(k, cr):
        got(ablk(cr, [u_y, u_sib, u_yx][k]), axs.at[k, cr], axr.at[k, cr])

    def out_cols(o, cc, h):
        return out.at[:, pl.ds(al(256 * (2 * o + cc) + 128 * h, 128), 128)]

    def pass_copy(h, o, cr):
        return rcopy(outb.at[h, o, cr], out_cols(o, c, h), ps.at[h, o, cr], pr.at[h, o, c], NX[cr])

    def project(cr, h, n, dy, dz):
        def step(i, carry):
            o = own(dy(i), dz(i))
            v = jnp.dot(att[r256(cr), :], wob[h, o], preferred_element_type=F32)
            r = v + hf[cr, o, :, 128 * h:128 * h + 128].astype(F32)
            outb[h, o, cr] = r.astype(BF)
            if cr == 1:
                pass_copy(h, o, cr).start()
            else:
                @pl.when(jnp.logical_not(wrap))
                def _():
                    pass_copy(h, o, cr).start()

                @pl.when(wrap)
                def _():
                    rcopy(outb.at[h, o, cr], rly.at[h, o], ps.at[h, o, cr], rr.at[h, o], MID).start()

            return carry

        lax.fori_loop(0, n, step, 0)

    def project_b(cr, h):
        project(cr, h, 4, lambda i: 0, lambda i: i)
        project(cr, h, 1, lambda i: 1, lambda i: 0)

    def project_c(cr, h):
        project(cr, h, 2, lambda i: 1, lambda i: 1 + 2 * i)

    def project_d(cr, h):
        project(cr, h, 1, lambda i: 1, lambda i: 2)

    def relay_copy(h, o):
        return rcopy(rly.at[h, o], out_cols(o, c, h), rs.at[h, o], pr.at[h, o, c], FAR[0])

    def relay(h, n, dy, dz):
        @pl.when(wrap)
        def _():
            def step(i, carry):
                o = own(dy(i), dz(i))
                got(rly.at[h, o], rs.at[h, o], rr.at[h, o])
                relay_copy(h, o).start()
                return carry

            lax.fori_loop(0, n, step, 0)

    def relay_b(h):
        relay(h, 4, lambda i: 0, lambda i: i)
        relay(h, 1, lambda i: 1, lambda i: 0)

    def relay_c(h):
        relay(h, 2, lambda i: 1, lambda i: 1 + 2 * i)

    def relay_d(h):
        relay(h, 1, lambda i: 1, lambda i: 2)

    attend(oy, 0, False)
    acopy(0, 0).start()
    o_zz(0)
    o_b2(1)
    attend(yh, 0, True)
    acopy(1, 0).start()
    agot(0, 0)
    acopy(2, 0).start()
    o_zz(1)
    for o in range(8):
        hid_local(o).wait()
        got(hf.at[oc, o], hs.at[o], hr.at[o])
    agot(1, 0)
    agot(2, 0)
    project_b(0, 0)
    attend(oy, 1, False)
    acopy(0, 1).start()
    o_c(0)
    project_c(0, 0)
    o_d(0)
    project_d(0, 0)
    project_b(0, 1)
    relay_b(0)
    attend(yh, 1, True)
    acopy(1, 1).start()
    agot(0, 1)
    acopy(2, 1).start()
    relay_c(0)
    relay_d(0)
    relay_b(1)
    agot(1, 1)
    agot(2, 1)
    project_b(1, 0)
    project_c(1, 0)
    project_d(1, 0)
    project_b(1, 1)
    o_c(1)
    project_c(0, 1)
    project_c(1, 1)
    o_d(1)
    project_d(0, 1)
    project_d(1, 1)
    relay_c(1)
    relay_d(1)

    for ci in range(4):
        for i in range(4):
            ring(ci, i).wait_send()
        if ci < KX:
            for n in range(3):
                fill(ci, n).wait_send()
    for h in (0, 1):
        for i in range(8):
            osend(h, i).wait_send()
    for n in range(3):
        segs(n).wait_send()
    for k in range(3):
        for q in range(4):
            xcopy(k, q).wait_send()
        for cr in (0, 1):
            acopy(k, cr).wait_send()
    for o in range(8):
        hid_remote(o).wait_send()
    for h in (0, 1):
        for o in range(8):
            for cc in (0, 1):
                pass_copy(h, o, cc).wait_send()
                got(out_cols(o, cc, h), ps.at[h, o, cc], pr.at[h, o, cc])

    @pl.when(wrap)
    def _():
        for h in (0, 1):
            for o in range(8):
                relay_copy(h, o).wait_send()


def body(section_input, segment_ids, query_weight, keyval_weight, out_weight):
    seg = segment_ids[0].astype(BF).reshape(2, 1, 128)
    seg = jnp.broadcast_to(seg, (2, 16, 128)).reshape(32, 128)
    wkv = keyval_weight[0].reshape(256, 2, 4, 64).transpose(0, 2, 1, 3).reshape(256, 512)
    vm = pl.BlockSpec(memory_space=pltpu.VMEM)
    hb = pl.BlockSpec(memory_space=pl.ANY)
    dma = pltpu.SemaphoreType.DMA
    res = pl.pallas_call(
        kernel,
        out_shape=jax.ShapeDtypeStruct((256, 4096), BF),
        in_specs=[vm, vm, hb, hb, hb],
        out_specs=hb,
        scratch_shapes=[
            pltpu.VMEM((4, 1024, 1024), BF),
            pltpu.VMEM((2, 4, 1024, 256), BF),
            pltpu.VMEM((4, 1024, 128), BF),
            pltpu.VMEM((2, 8, 2048, 128), BF),
            pltpu.VMEM((4, 1152, 128), BF),
            pltpu.VMEM((4, 1024, 128), BF),
            pltpu.VMEM((512, 2048), BF),
            pltpu.VMEM((2, 256, 512), BF),
            pltpu.VMEM((2, 8, 256, 256), BF),
            pltpu.VMEM((2, 8, 2, 256, 128), BF),
            pltpu.VMEM((2, 1024, 256), F32),
            pltpu.VMEM((1024, 128), F32),
            pltpu.VMEM((2, 256, 128), F32),
            pltpu.VMEM((4, 32, 128), BF),
            pltpu.VMEM((4, 256, 128), jnp.int32),
            dma((3, 3)), dma((3, 4)), dma((3,)),
            dma((4, 4)), dma((4, 4)),
            dma((2, 8)), dma((2, 8)), dma((2,)),
            dma((3, 4)), dma((3, 4)),
            dma((8,)), dma((8,)), dma((8,)),
            dma((3,)), dma((4,)),
            dma((3, 2)), dma((3, 2)),
            dma((2, 8, 2)), dma((2, 8, 2)),
            pltpu.VMEM((2, 8, 256, 128), BF),
            dma((2, 8)), dma((2, 8)),
        ],
        compiler_params=pltpu.CompilerParams(
            collective_id=0, has_side_effects=True, vmem_limit_bytes=58 << 20),
        name="layer",
    )(section_input[0], seg, query_weight[0], wkv, out_weight[0])
    return res[None]


def solution(mesh):
    fine = Mesh(mesh.devices.reshape(8, 2, 4, 2), ("section", "yh", "z", "core"))
    tok = ("yh", "z", "core")
    return jax.shard_map(
        body,
        mesh=fine,
        in_specs=(
            P("section", tok, None),
            P("section", tok),
            P("section", tok, None),
            P("section", tok, None),
            P("section", None, tok),
        ),
        out_specs=P("section", tok, None),
        check_vma=False,
    )
```

```python
import jax
import jax.numpy as jnp
from jax import lax
from jax.experimental import pallas as pl
from jax.experimental.pallas import tpu as pltpu
from jax.sharding import Mesh, PartitionSpec as P

BF = jnp.bfloat16
F32 = jnp.float32
MESH = pl.DeviceIdType.MESH
EXP_SCALE = 0.125 * 1.4426950408889634

KV, QA, QB, KA, KB = range(5)


def kernel(hid, seg, wq, wkv, wo, out,
           x, wqb, wkvb, wob, kvb, qs, att, atx, hf, outb, accq, acck, ostat, sgr, lod,
           fs, fr, fl, zs, zr, os_, or_, ol, xs, xr, hs, hr, hl, gs, gr, axs, axr, ps, pr):
    sec, yh, z, c = (lax.axis_index(n) for n in ("section", "yh", "z", "core"))
    oc, oy = 1 - c, 1 - yh
    u = 2 * yh + c
    u_sib, u_y, u_yx = 2 * yh + oc, 2 * oy + c, 2 * oy + oc
    b = yh * 4 + z
    zp, zm = (z + 1) % 4, (z + 3) % 4
    SIB = (sec, yh, z, oc)
    YP = (sec, oy, z, c)
    YX = (sec, oy, z, oc)
    ZP = (sec, yh, zp, c)
    ZM = (sec, yh, zm, c)
    nxt, prv = (sec + 1) % 8, (sec + 7) % 8
    NX = [(nxt, yh, z, 0), (nxt, yh, z, 1)]
    PV = [(prv, yh, z, 0), (prv, yh, z, 1)]

    def rcopy(src, dst, send, recv, dev):
        return pltpu.make_async_remote_copy(
            src_ref=src, dst_ref=dst, send_sem=send, recv_sem=recv,
            device_id=dev, device_id_type=MESH)

    def got(dst, send, recv):
        rcopy(dst, dst, send, recv, SIB).wait_recv()

    def al(v, n):
        return pl.multiple_of(v, n)

    def r256(k):
        return pl.ds(al(256 * k, 256), 256)

    bar = pltpu.get_barrier_semaphore()
    for d in [SIB, YP, YX, ZP, ZM] + NX + PV:
        pl.semaphore_signal(bar, inc=1, device_id=d, device_id_type=MESH)
    pl.semaphore_wait(bar, 9)

    def quarter(ci, v):
        if ci == KV:
            return wkv.at[:, pl.ds(al(128 * v, 128), 128)]
        return wq.at[:, pl.ds(al(512 * v + 256 * (ci - QA), 256), 256)]

    def rb(ci, zo):
        if ci == KV:
            return wkvb.at[zo]
        if ci == KA:
            return kvb.at[zo, yh]
        if ci == KB:
            return kvb.at[zo, oy, pl.ds(0, 512)]
        return wqb.at[ci - QA, zo]

    def fill(ci, n):
        v, dev = [(u_y, YP), (u_yx, YX), (u_sib, SIB)][n]
        return rcopy(quarter(ci, v), rb(ci, z).at[r256(u)], fs.at[ci, n], fr.at[ci, u], dev)

    def fill_local(ci):
        return pltpu.make_async_copy(quarter(ci, u), rb(ci, z).at[r256(u)], fl.at[ci])

    def fill_wait(ci):
        fill_local(ci).wait()
        for v in (u_sib, u_y, u_yx):
            got(rb(ci, z).at[r256(v)], fs.at[ci, 0], fr.at[ci, v])

    def rhalf(ci, zo, h):
        if ci == KB:
            return kvb.at[zo, oy, pl.ds(256 * h, 256)]
        n = 320 if ci == KA else 512
        return rb(ci, zo).at[pl.ds(n * h, n)]

    def ring(ci, i):
        src, dev = {
            0: lambda: (rb(ci, z), ZP),
            1: lambda: (rb(ci, z), ZM),
            2: lambda: (rhalf(ci, zm, 0), ZP),
            3: lambda: (rhalf(ci, zp, 1), ZM),
        }[i]()
        return rcopy(src, src, zs.at[ci, i], zr.at[ci, i], dev)

    def ring_got(ci, i):
        dst = {
            0: lambda: rb(ci, zm),
            1: lambda: rb(ci, zp),
            2: lambda: rhalf(ci, (z + 2) % 4, 0),
            3: lambda: rhalf(ci, (z + 2) % 4, 1),
        }[i]()
        got(dst, zs.at[ci, i], zr.at[ci, i])

    def ring_a(ci):
        ring(ci, 0).start()
        ring(ci, 1).start()

    def ring_b(ci):
        ring_got(ci, 0)
        ring(ci, 2).start()
        ring_got(ci, 1)
        ring(ci, 3).start()

    def ring_c(ci):
        ring_got(ci, 2)
        ring_got(ci, 3)

    def own(dy, dz):
        return ((yh + dy) % 2) * 4 + (z + dz) % 4

    def ob(h, dy, dz):
        return wob.at[h, own(dy, dz)]

    def oh(h, dy, dz, k):
        return wob.at[h, own(dy, dz), pl.ds(1024 * k, 1024)]

    def osend(h, i):
        src, dev = {
            0: lambda: (ob(h, 0, 0), YP),
            1: lambda: (ob(h, 0, 0), ZP),
            2: lambda: (ob(h, 0, 0), ZM),
            3: lambda: (ob(h, 1, 0), ZP),
            4: lambda: (ob(h, 1, 0), ZM),
            5: lambda: (oh(h, 0, 3, 0), ZP),
            6: lambda: (oh(h, 0, 1, 1), ZM),
            7: lambda: (oh(h, 1, 3, 0), ZP),
            8: lambda: (oh(h, 1, 1, 1), ZM),
        }[i]()
        return rcopy(src, src, os_.at[h, i], or_.at[h, i], dev)

    def ogot(h, i):
        dst = {
            0: lambda: ob(h, 1, 0),
            1: lambda: ob(h, 0, 3),
            2: lambda: ob(h, 0, 1),
            3: lambda: ob(h, 1, 3),
            4: lambda: ob(h, 1, 1),
            5: lambda: oh(h, 0, 2, 0),
            6: lambda: oh(h, 0, 2, 1),
            7: lambda: oh(h, 1, 2, 0),
            8: lambda: oh(h, 1, 2, 1),
        }[i]()
        got(dst, os_.at[h, i], or_.at[h, i])

    def o_fill(h):
        return pltpu.make_async_copy(wo.at[:, pl.ds(128 * h, 128)], wob.at[h, b], ol.at[h])

    def o_az(h):
        o_fill(h).wait()
        osend(h, 1).start()
        osend(h, 2).start()

    def o_ay(h):
        osend(h, 0).start()

    def o_b1(h):
        ogot(h, 1)
        osend(h, 5).start()
        ogot(h, 2)
        osend(h, 6).start()

    def o_b2(h):
        ogot(h, 0)
        osend(h, 3).start()
        osend(h, 4).start()

    def o_zz(h):
        ogot(h, 5)
        ogot(h, 6)

    def o_c(h):
        ogot(h, 3)
        osend(h, 7).start()
        ogot(h, 4)
        osend(h, 8).start()

    def o_d(h):
        ogot(h, 7)
        ogot(h, 8)

    for ci in (KV, QA, QB):
        for n in range(3):
            fill(ci, n).start()
        fill_local(ci).start()
    for h in (0, 1):
        o_fill(h).start()

    def segs(n):
        return rcopy(sgr.at[u], sgr.at[u], gs.at[n], gr.at[u], [YP, YX, SIB][n])

    sgr[u] = seg[...]
    for n in range(3):
        segs(n).start()

    def hid_cols(o, cc):
        return hid.at[:, pl.ds(al(256 * (2 * o + cc), 256), 256)]

    def hid_remote(o):
        return rcopy(hid_cols(o, oc), hf.at[c, o], hs.at[o], hr.at[o], SIB)

    def hid_local(o):
        return pltpu.make_async_copy(hid_cols(o, c), hf.at[c, o], hl.at[o])

    def norm(i, carry):
        r = pl.ds(al(32 * i, 32), 32)
        v = hid[r, :].astype(F32)
        v = v * lax.rsqrt(jnp.mean(v * v, axis=-1, keepdims=True) + 1e-05)
        v = v.astype(BF)
        dst = pl.ds(al(256 * u + 32 * i, 32), 32)
        for d in range(16):
            lanes = 256 * (2 * (d // 8) + d % 2)
            x[(d // 2) % 4, dst, lanes:lanes + 256] = v[:, 256 * d:256 * d + 256]
        return carry

    lax.fori_loop(0, 8, norm, 0)

    def xcopy(k, q):
        v, dev = [(u, YP), (u, SIB), (u_y, SIB)][k]
        ref = x.at[q, r256(v)]
        return rcopy(ref, ref, xs.at[k, q], xr.at[k, q], dev)

    def xgot(k, q):
        v = [u_y, u_sib, u_yx][k]
        got(x.at[q, r256(v)], xs.at[k, q], xr.at[k, q])

    for q in range(4):
        xcopy(0, q).start()
        xcopy(1, q).start()

    def x_forward(q):
        xgot(0, q)
        xcopy(2, q).start()

    acck[...] = jnp.zeros_like(acck)
    accq[...] = jnp.zeros_like(accq)

    def gemm(yr, lo, hi):
        rows = pl.ds(al(512 * yr, 512), 512)

        def step(q, carry):
            xv = x[q, rows, :]
            acck[rows, :] += jnp.dot(xv, wkvb[q], preferred_element_type=F32)
            for k in (0, 1):
                accq[k, rows, :] += jnp.dot(xv, wqb[k, q], preferred_element_type=F32)
            return carry

        lax.fori_loop(lo, hi, step, 0)

    for ci in (KV, QA, QB):
        fill_wait(ci)
        ring_a(ci)
    for o in range(8):
        hid_remote(o).start()
        hid_local(o).start()
    def keyvals_out(yr):
        kvb[z, yr, 0:512, :] = acck[pl.ds(al(512 * yr, 512), 512), :].astype(BF)

    def queries_out(yr):
        rows = pl.ds(al(512 * yr, 512), 512)
        for p in range(4):
            qs[p, rows, :] = accq[p // 2, rows, 128 * (p % 2):128 * (p % 2) + 128].astype(BF)

    ring_b(KV)
    x_forward(0)
    ring_b(QA)
    for q in range(4):
        xgot(1, q)
    x_forward(1)
    ring_b(QB)
    o_az(0)
    ring_c(KV)
    ring_c(QA)
    ring_c(QB)
    gemm(yh, 0, 4)
    keyvals_out(yh)
    for v in (u_sib, u_y, u_yx):
        got(sgr.at[v], gs.at[0], gr.at[v])
    for k in range(4):
        kvb[z, yh, 512 + 32 * k:544 + 32 * k, :] = sgr[k]
    ring_a(KA)
    x_forward(2)
    ring_b(KA)
    queries_out(yh)
    xgot(2, 0)
    xgot(2, 1)
    gemm(oy, 0, 2)
    xgot(2, 2)
    gemm(oy, 2, 3)
    ring_c(KA)
    o_b1(0)

    lane = lax.broadcasted_iota(jnp.int32, (256, 128), 1)
    row = lax.broadcasted_iota(jnp.int32, (256, 128), 0)
    low = lane < 64
    below1 = jnp.zeros((16, 128), F32)
    below2 = jnp.zeros((16, 128), F32)
    for q in range(4):
        for t in range(512, 640, 16):
            g = kvb[q, yh, t:t + 16, :].astype(F32)
            below1 = below1 + jnp.where(g < 0.5, 1.0, 0.0)
            below2 = below2 + jnp.where(g < 1.5, 1.0, 0.0)
    n1 = jnp.sum(below1[0:8], axis=-1, keepdims=True)[0:1, :]
    n2 = jnp.sum(below2[0:8], axis=-1, keepdims=True)[0:1, :]
    for r in range(4):
        g = jnp.concatenate(
            [jnp.transpose(jnp.broadcast_to(sgr[r, 16 * k:16 * k + 16, :].astype(F32)[0:1, :], (128, 128)))
             for k in (0, 1)], axis=0)
        start = jnp.where(g < 0.5, 0.0, jnp.where(g < 1.5, n1, n2)).astype(jnp.int32)
        pos = 2048 * (r // 2) + 512 * z + 256 * (r % 2) + row
        lod[r] = jnp.maximum(start, pos - 2047) - lane

    x_forward(3)
    o_ay(0)
    xgot(2, 3)
    gemm(oy, 3, 4)
    keyvals_out(oy)
    ring_a(KB)
    queries_out(oy)
    ring_b(KB)
    o_az(1)
    ring_c(KB)

    def attend(yr, cr, mine):
        r = 2 * yr + cr
        rblk = 2 * (4 * yr + z) + cr

        def one(p, carry):
            q2 = qs[p, r256(r), :].astype(F32)
            zero = jnp.zeros_like(q2)
            d1 = lod[r]
            for hh in (0, 1):
                q1 = jnp.where(low, q2 if hh == 0 else pltpu.roll(q2, 64, 1), zero).astype(BF)
                ss = []
                m = jnp.full((256, 128), -1e30, F32)
                for t in range(9):
                    kb = (rblk + t + 8) % 16
                    kk = kvb[(kb // 2) % 4, kb // 8, r256(kb % 2), :]
                    s = lax.dot_general(q1, kk, (((1,), (1,)), ((), ())),
                                        preferred_element_type=F32)
                    base = 256 * (rblk + t) - 2048
                    for v in (0, 1):
                        ok = d1 <= base + 128 * v
                        if t == 8:
                            ok = ok & (row - lane >= 128 * v)
                        su = jnp.where(ok, s[:, 128 * v:128 * v + 128], -1e30)
                        ss.append(su)
                        m = jnp.maximum(m, su)
                mm = jnp.max(m, axis=-1, keepdims=True)
                l = jnp.zeros((256, 128), F32)
                o_ = jnp.zeros((256, 128), F32)
                for t in range(9):
                    kb = (rblk + t + 8) % 16
                    kk = kvb[(kb // 2) % 4, kb // 8, r256(kb % 2), :]
                    w0 = jnp.exp2((ss[2 * t] - mm) * EXP_SCALE)
                    w1 = jnp.exp2((ss[2 * t + 1] - mm) * EXP_SCALE)
                    l = l + w0 + w1
                    o_ = o_ + jnp.dot(jnp.concatenate([w0, w1], axis=1).astype(BF), kk,
                                      preferred_element_type=F32)
                ostat[hh] = o_ / jnp.sum(l, axis=-1, keepdims=True)
            res = jnp.where(low, pltpu.roll(ostat[0], 64, 1), ostat[1]).astype(BF)
            if mine:
                att[r256(cr), pl.ds(al(512 * u + 128 * p, 128), 128)] = res
            else:
                atx[cr, :, pl.ds(al(128 * p, 128), 128)] = res
            return carry

        lax.fori_loop(0, 4, one, 0, unroll=2)

    def ablk(cr, v):
        return att.at[r256(cr), pl.ds(al(512 * v, 512), 512)]

    def acopy(k, cr):
        src, dst, dev = [
            lambda: (atx.at[cr], ablk(cr, u), YP),
            lambda: (ablk(cr, u), ablk(cr, u), SIB),
            lambda: (ablk(cr, u_y), ablk(cr, u_y), SIB),
        ][k]()
        return rcopy(src, dst, axs.at[k, cr], axr.at[k, cr], dev)

    def agot(k, cr):
        got(ablk(cr, [u_y, u_sib, u_yx][k]), axs.at[k, cr], axr.at[k, cr])

    def out_cols(o, cc, h):
        return out.at[:, pl.ds(al(256 * (2 * o + cc) + 128 * h, 128), 128)]

    def pass_copy(h, o, cr):
        return rcopy(outb.at[h, o, cr], out_cols(o, c, h), ps.at[h, o, cr], pr.at[h, o, c], NX[cr])

    def project(cr, h, n, dy, dz):
        def step(i, carry):
            o = own(dy(i), dz(i))
            v = jnp.dot(att[r256(cr), :], wob[h, o], preferred_element_type=F32)
            r = v + hf[cr, o, :, 128 * h:128 * h + 128].astype(F32)
            outb[h, o, cr] = r.astype(BF)
            pass_copy(h, o, cr).start()
            return carry

        lax.fori_loop(0, n, step, 0)

    def project_b(cr, h):
        project(cr, h, 4, lambda i: 0, lambda i: i)
        project(cr, h, 1, lambda i: 1, lambda i: 0)

    def project_c(cr, h):
        project(cr, h, 2, lambda i: 1, lambda i: 1 + 2 * i)

    def project_d(cr, h):
        project(cr, h, 1, lambda i: 1, lambda i: 2)

    attend(oy, 0, False)
    acopy(0, 0).start()
    o_ay(1)
    o_b2(0)
    attend(oy, 1, False)
    acopy(0, 1).start()
    o_b1(1)
    agot(0, 0)
    acopy(2, 0).start()
    for o in range(8):
        hid_local(o).wait()
        got(hf.at[oc, o], hs.at[o], hr.at[o])
    attend(yh, 0, True)
    acopy(1, 0).start()
    agot(0, 1)
    acopy(2, 1).start()
    o_b2(1)
    o_c(0)
    o_zz(0)
    agot(1, 0)
    agot(2, 0)
    project_b(0, 0)
    project_c(0, 0)
    o_zz(1)
    attend(yh, 1, True)
    acopy(1, 1).start()
    project_b(0, 1)
    agot(1, 1)
    agot(2, 1)
    project_b(1, 0)
    project_c(1, 0)
    o_c(1)
    project_b(1, 1)
    project_c(0, 1)
    project_c(1, 1)
    o_d(0)
    project_d(0, 0)
    project_d(1, 0)
    o_d(1)
    project_d(0, 1)
    project_d(1, 1)

    for ci in range(5):
        for i in range(4):
            ring(ci, i).wait_send()
        if ci < KA:
            for n in range(3):
                fill(ci, n).wait_send()
    for h in (0, 1):
        for i in range(9):
            osend(h, i).wait_send()
    for n in range(3):
        segs(n).wait_send()
    for k in range(3):
        for q in range(4):
            xcopy(k, q).wait_send()
        for cr in (0, 1):
            acopy(k, cr).wait_send()
    for o in range(8):
        hid_remote(o).wait_send()
    for h in (0, 1):
        for o in range(8):
            for cc in (0, 1):
                pass_copy(h, o, cc).wait_send()
                got(out_cols(o, cc, h), ps.at[h, o, cc], pr.at[h, o, cc])


def body(section_input, segment_ids, query_weight, keyval_weight, out_weight):
    seg = segment_ids[0].astype(BF).reshape(2, 1, 128)
    seg = jnp.broadcast_to(seg, (2, 16, 128)).reshape(32, 128)
    wkv = keyval_weight[0].reshape(256, 2, 4, 64).transpose(0, 2, 1, 3).reshape(256, 512)
    vm = pl.BlockSpec(memory_space=pltpu.VMEM)
    hb = pl.BlockSpec(memory_space=pl.ANY)
    dma = pltpu.SemaphoreType.DMA
    res = pl.pallas_call(
        kernel,
        out_shape=jax.ShapeDtypeStruct((256, 4096), BF),
        in_specs=[vm, vm, hb, hb, hb],
        out_specs=hb,
        scratch_shapes=[
            pltpu.VMEM((4, 1024, 1024), BF),
            pltpu.VMEM((2, 4, 1024, 256), BF),
            pltpu.VMEM((4, 1024, 128), BF),
            pltpu.VMEM((2, 8, 2048, 128), BF),
            pltpu.VMEM((4, 2, 640, 128), BF),
            pltpu.VMEM((4, 1024, 128), BF),
            pltpu.VMEM((512, 2048), BF),
            pltpu.VMEM((2, 256, 512), BF),
            pltpu.VMEM((2, 8, 256, 256), BF),
            pltpu.VMEM((2, 8, 2, 256, 128), BF),
            pltpu.VMEM((2, 1024, 256), F32),
            pltpu.VMEM((1024, 128), F32),
            pltpu.VMEM((2, 256, 128), F32),
            pltpu.VMEM((4, 32, 128), BF),
            pltpu.VMEM((4, 256, 128), jnp.int32),
            dma((3, 3)), dma((3, 4)), dma((3,)),
            dma((5, 4)), dma((5, 4)),
            dma((2, 9)), dma((2, 9)), dma((2,)),
            dma((3, 4)), dma((3, 4)),
            dma((8,)), dma((8,)), dma((8,)),
            dma((3,)), dma((4,)),
            dma((3, 2)), dma((3, 2)),
            dma((2, 8, 2)), dma((2, 8, 2)),
        ],
        compiler_params=pltpu.CompilerParams(
            collective_id=0, has_side_effects=True, vmem_limit_bytes=58 << 20),
        name="layer",
    )(section_input[0], seg, query_weight[0], wkv, out_weight[0])
    return res[None]


def solution(mesh):
    fine = Mesh(mesh.devices.reshape(8, 2, 4, 2), ("section", "yh", "z", "core"))
    tok = ("yh", "z", "core")
    return jax.shard_map(
        body,
        mesh=fine,
        in_specs=(
            P("section", tok, None),
            P("section", tok),
            P("section", tok, None),
            P("section", tok, None),
            P("section", None, tok),
        ),
        out_specs=P("section", tok, None),
        check_vma=False,
    )
```

```python
import jax
import jax.numpy as jnp
from jax import lax
from jax.experimental import pallas as pl
from jax.experimental.pallas import tpu as pltpu
from jax.sharding import Mesh, PartitionSpec as P

BF = jnp.bfloat16
F32 = jnp.float32
MESH = pl.DeviceIdType.MESH
EXP_SCALE = 0.125 * 1.4426950408889634

KV, QA, QB, KA, KB = range(5)


def kernel(hid, seg, wq, wkv, wo, out,
           x, wqb, wkvb, wob, kvb, qs, att, atx, hf, outb, accq, acck, ostat, sgr, lod, wkr,
           fs, fr, fl, zs, zr, os_, or_, ol, xs, xr, hs, hr, hl, gs, gr, axs, axr, ps, pr):
    sec, yh, z, c = (lax.axis_index(n) for n in ("section", "yh", "z", "core"))
    oc, oy = 1 - c, 1 - yh
    u = 2 * yh + c
    u_sib, u_y, u_yx = 2 * yh + oc, 2 * oy + c, 2 * oy + oc
    b = yh * 4 + z
    zp, zm = (z + 1) % 4, (z + 3) % 4
    SIB = (sec, yh, z, oc)
    YP = (sec, oy, z, c)
    YX = (sec, oy, z, oc)
    ZP = (sec, yh, zp, c)
    ZM = (sec, yh, zm, c)
    nxt, prv = (sec + 1) % 8, (sec + 7) % 8
    NX = [(nxt, yh, z, 0), (nxt, yh, z, 1)]
    PV = [(prv, yh, z, 0), (prv, yh, z, 1)]

    def rcopy(src, dst, send, recv, dev):
        return pltpu.make_async_remote_copy(
            src_ref=src, dst_ref=dst, send_sem=send, recv_sem=recv,
            device_id=dev, device_id_type=MESH)

    def got(dst, send, recv):
        rcopy(dst, dst, send, recv, SIB).wait_recv()

    def al(v, n):
        return pl.multiple_of(v, n)

    def r256(k):
        return pl.ds(al(256 * k, 256), 256)

    lane = lax.broadcasted_iota(jnp.int32, (256, 128), 1)
    row = lax.broadcasted_iota(jnp.int32, (256, 128), 0)
    low = lane < 64

    for j in (0, 1):
        kp = wkv[:, 128 * j:128 * j + 128].astype(F32)
        vp = wkv[:, 256 + 128 * j:384 + 128 * j].astype(F32)
        wkr[2 * j] = jnp.where(low, kp, pltpu.roll(vp, 64, 1)).astype(BF)
        wkr[2 * j + 1] = jnp.where(low, pltpu.roll(kp, 64, 1), vp).astype(BF)
    for k in (0, 1):
        part = jnp.broadcast_to(seg[0:1, 128 * k:128 * k + 128].astype(F32), (16, 128))
        sgr[u, 16 * k:16 * k + 16, :] = part.astype(BF)

    bar = pltpu.get_barrier_semaphore()
    for d in [SIB, YP, YX, ZP, ZM] + NX + PV:
        pl.semaphore_signal(bar, inc=1, device_id=d, device_id_type=MESH)
    pl.semaphore_wait(bar, 9)

    def quarter(ci, v):
        if ci == KV:
            return wkr.at[v]
        return wq.at[:, pl.ds(al(512 * v + 256 * (ci - QA), 256), 256)]

    def rb(ci, zo):
        if ci == KV:
            return wkvb.at[zo]
        if ci == KA:
            return kvb.at[zo, yh]
        if ci == KB:
            return kvb.at[zo, oy, pl.ds(0, 512)]
        return wqb.at[ci - QA, zo]

    def fill(ci, n):
        v, dev = [(u_y, YP), (u_yx, YX), (u_sib, SIB)][n]
        return rcopy(quarter(ci, v), rb(ci, z).at[r256(u)], fs.at[ci, n], fr.at[ci, u], dev)

    def fill_local(ci):
        return pltpu.make_async_copy(quarter(ci, u), rb(ci, z).at[r256(u)], fl.at[ci])

    def fill_wait(ci):
        fill_local(ci).wait()
        for v in (u_sib, u_y, u_yx):
            got(rb(ci, z).at[r256(v)], fs.at[ci, 0], fr.at[ci, v])

    def rhalf(ci, zo, h):
        if ci == KB:
            return kvb.at[zo, oy, pl.ds(256 * h, 256)]
        n = 320 if ci == KA else 512
        return rb(ci, zo).at[pl.ds(n * h, n)]

    def ring(ci, i):
        src, dev = {
            0: lambda: (rb(ci, z), ZP),
            1: lambda: (rb(ci, z), ZM),
            2: lambda: (rhalf(ci, zm, 0), ZP),
            3: lambda: (rhalf(ci, zp, 1), ZM),
        }[i]()
        return rcopy(src, src, zs.at[ci, i], zr.at[ci, i], dev)

    def ring_got(ci, i):
        dst = {
            0: lambda: rb(ci, zm),
            1: lambda: rb(ci, zp),
            2: lambda: rhalf(ci, (z + 2) % 4, 0),
            3: lambda: rhalf(ci, (z + 2) % 4, 1),
        }[i]()
        got(dst, zs.at[ci, i], zr.at[ci, i])

    def ring_a(ci):
        ring(ci, 0).start()
        ring(ci, 1).start()

    def ring_b(ci):
        ring_got(ci, 0)
        ring(ci, 2).start()
        ring_got(ci, 1)
        ring(ci, 3).start()

    def ring_c(ci):
        ring_got(ci, 2)
        ring_got(ci, 3)

    def own(dy, dz):
        return ((yh + dy) % 2) * 4 + (z + dz) % 4

    def ob(h, dy, dz):
        return wob.at[h, own(dy, dz)]

    def oh(h, dy, dz, k):
        return wob.at[h, own(dy, dz), pl.ds(1024 * k, 1024)]

    def osend(h, i):
        src, dev = {
            0: lambda: (ob(h, 0, 0), YP),
            1: lambda: (ob(h, 0, 0), ZP),
            2: lambda: (ob(h, 0, 0), ZM),
            3: lambda: (ob(h, 1, 0), ZP),
            4: lambda: (ob(h, 1, 0), ZM),
            5: lambda: (oh(h, 0, 3, 0), ZP),
            6: lambda: (oh(h, 0, 1, 1), ZM),
            7: lambda: (oh(h, 1, 3, 0), ZP),
            8: lambda: (oh(h, 1, 1, 1), ZM),
        }[i]()
        return rcopy(src, src, os_.at[h, i], or_.at[h, i], dev)

    def ogot(h, i):
        dst = {
            0: lambda: ob(h, 1, 0),
            1: lambda: ob(h, 0, 3),
            2: lambda: ob(h, 0, 1),
            3: lambda: ob(h, 1, 3),
            4: lambda: ob(h, 1, 1),
            5: lambda: oh(h, 0, 2, 0),
            6: lambda: oh(h, 0, 2, 1),
            7: lambda: oh(h, 1, 2, 0),
            8: lambda: oh(h, 1, 2, 1),
        }[i]()
        got(dst, os_.at[h, i], or_.at[h, i])

    def o_fill(h):
        return pltpu.make_async_copy(wo.at[:, pl.ds(128 * h, 128)], wob.at[h, b], ol.at[h])

    def o_az(h):
        o_fill(h).wait()
        osend(h, 1).start()
        osend(h, 2).start()

    def o_ay(h):
        osend(h, 0).start()

    def o_b1(h):
        ogot(h, 1)
        osend(h, 5).start()
        ogot(h, 2)
        osend(h, 6).start()

    def o_b2(h):
        ogot(h, 0)
        osend(h, 3).start()
        osend(h, 4).start()

    def o_zz(h):
        ogot(h, 5)
        ogot(h, 6)

    def o_c(h):
        ogot(h, 3)
        osend(h, 7).start()
        ogot(h, 4)
        osend(h, 8).start()

    def o_d(h):
        ogot(h, 7)
        ogot(h, 8)

    for ci in (KV, QA, QB):
        for n in range(3):
            fill(ci, n).start()
        fill_local(ci).start()
    for h in (0, 1):
        o_fill(h).start()

    def segs(n):
        return rcopy(sgr.at[u], sgr.at[u], gs.at[n], gr.at[u], [YP, YX, SIB][n])

    for n in range(3):
        segs(n).start()

    def hid_cols(o, cc):
        return hid.at[:, pl.ds(al(256 * (2 * o + cc), 256), 256)]

    def hid_remote(o):
        return rcopy(hid_cols(o, oc), hf.at[c, o], hs.at[o], hr.at[o], SIB)

    def hid_local(o):
        return pltpu.make_async_copy(hid_cols(o, c), hf.at[c, o], hl.at[o])

    def norm(i, carry):
        r = pl.ds(al(32 * i, 32), 32)
        v = hid[r, :].astype(F32)
        v = v * lax.rsqrt(jnp.mean(v * v, axis=-1, keepdims=True) + 1e-05)
        v = v.astype(BF)
        dst = pl.ds(al(256 * u + 32 * i, 32), 32)
        for d in range(16):
            lanes = 256 * (2 * (d // 8) + d % 2)
            x[(d // 2) % 4, dst, lanes:lanes + 256] = v[:, 256 * d:256 * d + 256]
        return carry

    lax.fori_loop(0, 8, norm, 0)

    def xcopy(k, q):
        v, dev = [(u, YP), (u, SIB), (u_y, SIB)][k]
        ref = x.at[q, r256(v)]
        return rcopy(ref, ref, xs.at[k, q], xr.at[k, q], dev)

    def xgot(k, q):
        v = [u_y, u_sib, u_yx][k]
        got(x.at[q, r256(v)], xs.at[k, q], xr.at[k, q])

    for q in range(4):
        xcopy(0, q).start()
        xcopy(1, q).start()

    def x_forward(q):
        xgot(0, q)
        xcopy(2, q).start()

    acck[...] = jnp.zeros_like(acck)
    accq[...] = jnp.zeros_like(accq)

    def gemm(yr, lo, hi):
        rows = pl.ds(al(512 * yr, 512), 512)

        def step(q, carry):
            xv = x[q, rows, :]
            acck[rows, :] += jnp.dot(xv, wkvb[q], preferred_element_type=F32)
            for k in (0, 1):
                accq[k, rows, :] += jnp.dot(xv, wqb[k, q], preferred_element_type=F32)
            return carry

        lax.fori_loop(lo, hi, step, 0)

    for ci in (KV, QA, QB):
        fill_wait(ci)
        ring_a(ci)
    for o in range(8):
        hid_remote(o).start()
        hid_local(o).start()
    def keyvals_out(yr):
        kvb[z, yr, 0:512, :] = acck[pl.ds(al(512 * yr, 512), 512), :].astype(BF)

    def queries_out(yr):
        rows = pl.ds(al(512 * yr, 512), 512)
        for p in range(4):
            qs[p, rows, :] = accq[p // 2, rows, 128 * (p % 2):128 * (p % 2) + 128].astype(BF)

    ring_b(KV)
    x_forward(0)
    ring_b(QA)
    for q in range(4):
        xgot(1, q)
    x_forward(1)
    ring_b(QB)
    o_az(0)
    ring_c(KV)
    ring_c(QA)
    ring_c(QB)
    gemm(yh, 0, 4)
    keyvals_out(yh)
    for v in (u_sib, u_y, u_yx):
        got(sgr.at[v], gs.at[0], gr.at[v])
    for k in range(4):
        kvb[z, yh, 512 + 32 * k:544 + 32 * k, :] = sgr[k]
    ring_a(KA)
    x_forward(2)
    ring_b(KA)
    queries_out(yh)
    xgot(2, 0)
    xgot(2, 1)
    gemm(oy, 0, 2)
    xgot(2, 2)
    gemm(oy, 2, 3)
    ring_c(KA)
    o_b1(0)

    below1 = jnp.zeros((16, 128), F32)
    below2 = jnp.zeros((16, 128), F32)
    for q in range(4):
        for t in range(512, 640, 16):
            g = kvb[q, yh, t:t + 16, :].astype(F32)
            below1 = below1 + jnp.where(g < 0.5, 1.0, 0.0)
            below2 = below2 + jnp.where(g < 1.5, 1.0, 0.0)
    n1 = jnp.sum(below1[0:8], axis=-1, keepdims=True)[0:1, :]
    n2 = jnp.sum(below2[0:8], axis=-1, keepdims=True)[0:1, :]
    for r in range(4):
        g = jnp.concatenate(
            [jnp.transpose(jnp.broadcast_to(sgr[r, 16 * k:16 * k + 16, :].astype(F32)[0:1, :], (128, 128)))
             for k in (0, 1)], axis=0)
        start = jnp.where(g < 0.5, 0.0, jnp.where(g < 1.5, n1, n2)).astype(jnp.int32)
        pos = 2048 * (r // 2) + 512 * z + 256 * (r % 2) + row
        lod[r] = jnp.maximum(start, pos - 2047) - lane

    x_forward(3)
    o_ay(0)
    xgot(2, 3)
    gemm(oy, 3, 4)
    keyvals_out(oy)
    ring_a(KB)
    queries_out(oy)
    ring_b(KB)
    o_az(1)
    ring_c(KB)

    def attend(yr, cr, mine):
        r = 2 * yr + cr
        rblk = 2 * (4 * yr + z) + cr

        def one(p, carry):
            q2 = qs[p, r256(r), :].astype(F32)
            zero = jnp.zeros_like(q2)
            d1 = lod[r]
            for hh in (0, 1):
                q1 = jnp.where(low, q2 if hh == 0 else pltpu.roll(q2, 64, 1), zero).astype(BF)
                ss = []
                m = jnp.full((256, 128), -1e30, F32)
                for t in range(9):
                    kb = (rblk + t + 8) % 16
                    kk = kvb[(kb // 2) % 4, kb // 8, r256(kb % 2), :]
                    s = lax.dot_general(q1, kk, (((1,), (1,)), ((), ())),
                                        preferred_element_type=F32)
                    base = 256 * (rblk + t) - 2048
                    for v in (0, 1):
                        ok = d1 <= base + 128 * v
                        if t == 8:
                            ok = ok & (row - lane >= 128 * v)
                        su = jnp.where(ok, s[:, 128 * v:128 * v + 128], -1e30)
                        ss.append(su)
                        m = jnp.maximum(m, su)
                mm = jnp.max(m, axis=-1, keepdims=True)
                l = jnp.zeros((256, 128), F32)
                o_ = jnp.zeros((256, 128), F32)
                for t in range(9):
                    kb = (rblk + t + 8) % 16
                    kk = kvb[(kb // 2) % 4, kb // 8, r256(kb % 2), :]
                    w0 = jnp.exp2((ss[2 * t] - mm) * EXP_SCALE)
                    w1 = jnp.exp2((ss[2 * t + 1] - mm) * EXP_SCALE)
                    l = l + w0 + w1
                    o_ = o_ + jnp.dot(jnp.concatenate([w0, w1], axis=1).astype(BF), kk,
                                      preferred_element_type=F32)
                ostat[hh] = o_ / jnp.sum(l, axis=-1, keepdims=True)
            res = jnp.where(low, pltpu.roll(ostat[0], 64, 1), ostat[1]).astype(BF)
            if mine:
                att[r256(cr), pl.ds(al(512 * u + 128 * p, 128), 128)] = res
            else:
                atx[cr, :, pl.ds(al(128 * p, 128), 128)] = res
            return carry

        lax.fori_loop(0, 4, one, 0, unroll=2)

    def ablk(cr, v):
        return att.at[r256(cr), pl.ds(al(512 * v, 512), 512)]

    def acopy(k, cr):
        src, dst, dev = [
            lambda: (atx.at[cr], ablk(cr, u), YP),
            lambda: (ablk(cr, u), ablk(cr, u), SIB),
            lambda: (ablk(cr, u_y), ablk(cr, u_y), SIB),
        ][k]()
        return rcopy(src, dst, axs.at[k, cr], axr.at[k, cr], dev)

    def agot(k, cr):
        got(ablk(cr, [u_y, u_sib, u_yx][k]), axs.at[k, cr], axr.at[k, cr])

    def out_cols(o, cc, h):
        return out.at[:, pl.ds(al(256 * (2 * o + cc) + 128 * h, 128), 128)]

    def pass_copy(h, o, cr):
        return rcopy(outb.at[h, o, cr], out_cols(o, c, h), ps.at[h, o, cr], pr.at[h, o, c], NX[cr])

    def project(cr, h, n, dy, dz):
        def step(i, carry):
            o = own(dy(i), dz(i))
            v = jnp.dot(att[r256(cr), :], wob[h, o], preferred_element_type=F32)
            r = v + hf[cr, o, :, 128 * h:128 * h + 128].astype(F32)
            outb[h, o, cr] = r.astype(BF)
            pass_copy(h, o, cr).start()
            return carry

        lax.fori_loop(0, n, step, 0)

    def project_b(cr, h):
        project(cr, h, 3, lambda i: 0, lambda i: i + i // 2)
        project(cr, h, 1, lambda i: 1, lambda i: 0)

    def project_z(cr, h):
        project(cr, h, 1, lambda i: 0, lambda i: 2)

    def project_c(cr, h):
        project(cr, h, 2, lambda i: 1, lambda i: 1 + 2 * i)

    def project_d(cr, h):
        project(cr, h, 1, lambda i: 1, lambda i: 2)

    attend(oy, 0, False)
    acopy(0, 0).start()
    o_ay(1)
    o_b2(0)
    attend(oy, 1, False)
    acopy(0, 1).start()
    o_b1(1)
    agot(0, 0)
    acopy(2, 0).start()
    for o in range(8):
        hid_local(o).wait()
        got(hf.at[oc, o], hs.at[o], hr.at[o])
    attend(yh, 0, True)
    acopy(1, 0).start()
    agot(0, 1)
    acopy(2, 1).start()
    o_zz(0)
    agot(1, 0)
    agot(2, 0)
    project_b(0, 0)
    o_c(0)
    o_b2(1)
    project_z(0, 0)
    project_c(0, 0)
    project_b(0, 1)
    attend(yh, 1, True)
    acopy(1, 1).start()
    o_zz(1)
    project_z(0, 1)
    agot(1, 1)
    agot(2, 1)
    project_b(1, 0)
    project_z(1, 0)
    project_c(1, 0)
    project_b(1, 1)
    project_z(1, 1)
    o_c(1)
    o_d(0)
    project_d(0, 0)
    project_d(1, 0)
    project_c(0, 1)
    project_c(1, 1)
    o_d(1)
    project_d(0, 1)
    project_d(1, 1)

    for ci in range(5):
        for i in range(4):
            ring(ci, i).wait_send()
        if ci < KA:
            for n in range(3):
                fill(ci, n).wait_send()
    for h in (0, 1):
        for i in range(9):
            osend(h, i).wait_send()
    for n in range(3):
        segs(n).wait_send()
    for k in range(3):
        for q in range(4):
            xcopy(k, q).wait_send()
        for cr in (0, 1):
            acopy(k, cr).wait_send()
    for o in range(8):
        hid_remote(o).wait_send()
    for h in (0, 1):
        for o in range(8):
            for cc in (0, 1):
                pass_copy(h, o, cc).wait_send()
                got(out_cols(o, cc, h), ps.at[h, o, cc], pr.at[h, o, cc])


def body(section_input, segment_ids, query_weight, keyval_weight, out_weight):
    vm = pl.BlockSpec(memory_space=pltpu.VMEM)
    hb = pl.BlockSpec(memory_space=pl.ANY)
    dma = pltpu.SemaphoreType.DMA
    res = pl.pallas_call(
        kernel,
        out_shape=jax.ShapeDtypeStruct((256, 4096), BF),
        in_specs=[vm, vm, hb, vm, hb],
        out_specs=hb,
        scratch_shapes=[
            pltpu.VMEM((4, 1024, 1024), BF),
            pltpu.VMEM((2, 4, 1024, 256), BF),
            pltpu.VMEM((4, 1024, 128), BF),
            pltpu.VMEM((2, 8, 2048, 128), BF),
            pltpu.VMEM((4, 2, 640, 128), BF),
            pltpu.VMEM((4, 1024, 128), BF),
            pltpu.VMEM((512, 2048), BF),
            pltpu.VMEM((2, 256, 512), BF),
            pltpu.VMEM((2, 8, 256, 256), BF),
            pltpu.VMEM((2, 8, 2, 256, 128), BF),
            pltpu.VMEM((2, 1024, 256), F32),
            pltpu.VMEM((1024, 128), F32),
            pltpu.VMEM((2, 256, 128), F32),
            pltpu.VMEM((4, 32, 128), BF),
            pltpu.VMEM((4, 256, 128), jnp.int32),
            pltpu.VMEM((4, 256, 128), BF),
            dma((3, 3)), dma((3, 4)), dma((3,)),
            dma((5, 4)), dma((5, 4)),
            dma((2, 9)), dma((2, 9)), dma((2,)),
            dma((3, 4)), dma((3, 4)),
            dma((8,)), dma((8,)), dma((8,)),
            dma((3,)), dma((4,)),
            dma((3, 2)), dma((3, 2)),
            dma((2, 8, 2)), dma((2, 8, 2)),
        ],
        compiler_params=pltpu.CompilerParams(
            collective_id=0, has_side_effects=True, vmem_limit_bytes=58 << 20),
        name="layer",
    )(section_input[0], segment_ids, query_weight[0], keyval_weight[0], out_weight[0])
    return res[None]


def solution(mesh):
    fine = Mesh(mesh.devices.reshape(8, 2, 4, 2), ("section", "yh", "z", "core"))
    tok = ("yh", "z", "core")
    return jax.shard_map(
        body,
        mesh=fine,
        in_specs=(
            P("section", tok, None),
            P("section", tok),
            P("section", tok, None),
            P("section", tok, None),
            P("section", None, tok),
        ),
        out_specs=P("section", tok, None),
        check_vma=False,
    )
```

```python
import jax
import jax.numpy as jnp
from jax import lax
from jax.experimental import pallas as pl
from jax.experimental.pallas import tpu as pltpu
from jax.sharding import Mesh, PartitionSpec as P

BF = jnp.bfloat16
F32 = jnp.float32
MESH = pl.DeviceIdType.MESH
EXP_SCALE = 0.125 * 1.4426950408889634

KV, QA, QB, KA, KB = range(5)


def kernel(hid, seg, wq, wkv, wo, out,
           x, wqb, wkvb, wob, kvb, qs, att, atx, hf, outb, accq, acck, ostat, sgr, lod, wkr,
           fs, fr, fl, zs, zr, os_, or_, ol, xs, xr, hs, hr, hl, gs, gr, axs, axr, ps, pr):
    sec, yh, z, c = (lax.axis_index(n) for n in ("section", "yh", "z", "core"))
    oc, oy = 1 - c, 1 - yh
    u = 2 * yh + c
    u_sib, u_y, u_yx = 2 * yh + oc, 2 * oy + c, 2 * oy + oc
    b = yh * 4 + z
    zp, zm = (z + 1) % 4, (z + 3) % 4
    SIB = (sec, yh, z, oc)
    YP = (sec, oy, z, c)
    YX = (sec, oy, z, oc)
    ZP = (sec, yh, zp, c)
    ZM = (sec, yh, zm, c)
    nxt, prv = (sec + 1) % 8, (sec + 7) % 8
    NX = [(nxt, yh, z, 0), (nxt, yh, z, 1)]
    PV = [(prv, yh, z, 0), (prv, yh, z, 1)]

    def rcopy(src, dst, send, recv, dev):
        return pltpu.make_async_remote_copy(
            src_ref=src, dst_ref=dst, send_sem=send, recv_sem=recv,
            device_id=dev, device_id_type=MESH)

    def got(dst, send, recv):
        rcopy(dst, dst, send, recv, SIB).wait_recv()

    def al(v, n):
        return pl.multiple_of(v, n)

    def r256(k):
        return pl.ds(al(256 * k, 256), 256)

    lane = lax.broadcasted_iota(jnp.int32, (256, 128), 1)
    row = lax.broadcasted_iota(jnp.int32, (256, 128), 0)
    low = lane < 64

    for j in (0, 1):
        kp = wkv[:, 128 * j:128 * j + 128].astype(F32)
        vp = wkv[:, 256 + 128 * j:384 + 128 * j].astype(F32)
        wkr[2 * j] = jnp.where(low, kp, pltpu.roll(vp, 64, 1)).astype(BF)
        wkr[2 * j + 1] = jnp.where(low, pltpu.roll(kp, 64, 1), vp).astype(BF)
    for k in (0, 1):
        part = jnp.broadcast_to(seg[0:1, 128 * k:128 * k + 128].astype(F32), (16, 128))
        sgr[u, 16 * k:16 * k + 16, :] = part.astype(BF)

    bar = pltpu.get_barrier_semaphore()
    for d in [SIB, YP, YX, ZP, ZM] + NX + PV:
        pl.semaphore_signal(bar, inc=1, device_id=d, device_id_type=MESH)
    pl.semaphore_wait(bar, 9)

    def quarter(ci, v):
        if ci == KV:
            return wkr.at[v]
        return wq.at[:, pl.ds(al(512 * v + 256 * (ci - QA), 256), 256)]

    def rb(ci, zo):
        if ci == KV:
            return wkvb.at[zo]
        if ci == KA:
            return kvb.at[zo, yh]
        if ci == KB:
            return kvb.at[zo, oy, pl.ds(0, 512)]
        return wqb.at[ci - QA, zo]

    def fill(ci, n):
        v, dev = [(u_y, YP), (u_yx, YX), (u_sib, SIB)][n]
        return rcopy(quarter(ci, v), rb(ci, z).at[r256(u)], fs.at[ci, n], fr.at[ci, u], dev)

    def fill_local(ci):
        return pltpu.make_async_copy(quarter(ci, u), rb(ci, z).at[r256(u)], fl.at[ci])

    def fill_wait(ci):
        fill_local(ci).wait()
        for v in (u_sib, u_y, u_yx):
            got(rb(ci, z).at[r256(v)], fs.at[ci, 0], fr.at[ci, v])

    def rhalf(ci, zo, h):
        if ci == KB:
            return kvb.at[zo, oy, pl.ds(256 * h, 256)]
        n = 320 if ci == KA else 512
        return rb(ci, zo).at[pl.ds(n * h, n)]

    def ring(ci, i):
        src, dev = {
            0: lambda: (rb(ci, z), ZP),
            1: lambda: (rb(ci, z), ZM),
            2: lambda: (rhalf(ci, zm, 0), ZP),
            3: lambda: (rhalf(ci, zp, 1), ZM),
        }[i]()
        return rcopy(src, src, zs.at[ci, i], zr.at[ci, i], dev)

    def ring_got(ci, i):
        dst = {
            0: lambda: rb(ci, zm),
            1: lambda: rb(ci, zp),
            2: lambda: rhalf(ci, (z + 2) % 4, 0),
            3: lambda: rhalf(ci, (z + 2) % 4, 1),
        }[i]()
        got(dst, zs.at[ci, i], zr.at[ci, i])

    def ring_a(ci):
        ring(ci, 0).start()
        ring(ci, 1).start()

    def ring_b(ci):
        ring_got(ci, 0)
        ring(ci, 2).start()
        ring_got(ci, 1)
        ring(ci, 3).start()

    def ring_c(ci):
        ring_got(ci, 2)
        ring_got(ci, 3)

    def own(dy, dz):
        return ((yh + dy) % 2) * 4 + (z + dz) % 4

    def ob(h, dy, dz):
        return wob.at[h, own(dy, dz)]

    def oh(h, dy, dz, k):
        return wob.at[h, own(dy, dz), pl.ds(1024 * k, 1024)]

    def osend(h, i):
        src, dev = {
            0: lambda: (ob(h, 0, 0), YP),
            1: lambda: (ob(h, 0, 0), ZP),
            2: lambda: (ob(h, 0, 0), ZM),
            3: lambda: (ob(h, 1, 0), ZP),
            4: lambda: (ob(h, 1, 0), ZM),
            5: lambda: (oh(h, 0, 3, 0), ZP),
            6: lambda: (oh(h, 0, 1, 1), ZM),
            7: lambda: (oh(h, 1, 3, 0), ZP),
            8: lambda: (oh(h, 1, 1, 1), ZM),
        }[i]()
        return rcopy(src, src, os_.at[h, i], or_.at[h, i], dev)

    def ogot(h, i):
        dst = {
            0: lambda: ob(h, 1, 0),
            1: lambda: ob(h, 0, 3),
            2: lambda: ob(h, 0, 1),
            3: lambda: ob(h, 1, 3),
            4: lambda: ob(h, 1, 1),
            5: lambda: oh(h, 0, 2, 0),
            6: lambda: oh(h, 0, 2, 1),
            7: lambda: oh(h, 1, 2, 0),
            8: lambda: oh(h, 1, 2, 1),
        }[i]()
        got(dst, os_.at[h, i], or_.at[h, i])

    def o_fill(h):
        return pltpu.make_async_copy(wo.at[:, pl.ds(128 * h, 128)], wob.at[h, b], ol.at[h])

    def o_az(h):
        o_fill(h).wait()
        osend(h, 1).start()
        osend(h, 2).start()

    def o_ay(h):
        osend(h, 0).start()

    def o_b1(h):
        ogot(h, 1)
        osend(h, 5).start()
        ogot(h, 2)
        osend(h, 6).start()

    def o_b2(h):
        ogot(h, 0)
        osend(h, 3).start()
        osend(h, 4).start()

    def o_zz(h):
        ogot(h, 5)
        ogot(h, 6)

    def o_c(h):
        ogot(h, 3)
        osend(h, 7).start()
        ogot(h, 4)
        osend(h, 8).start()

    def o_d(h):
        ogot(h, 7)
        ogot(h, 8)

    for ci in (KV, QA, QB):
        for n in range(3):
            fill(ci, n).start()
        fill_local(ci).start()
    for h in (0, 1):
        o_fill(h).start()

    def segs(n):
        return rcopy(sgr.at[u], sgr.at[u], gs.at[n], gr.at[u], [YP, YX, SIB][n])

    for n in range(3):
        segs(n).start()

    def hid_cols(o, cc):
        return hid.at[:, pl.ds(al(256 * (2 * o + cc), 256), 256)]

    def hid_remote(o):
        return rcopy(hid_cols(o, oc), hf.at[c, o], hs.at[o], hr.at[o], SIB)

    def hid_local(o):
        return pltpu.make_async_copy(hid_cols(o, c), hf.at[c, o], hl.at[o])

    def norm(i, carry):
        r = pl.ds(al(32 * i, 32), 32)
        v = hid[r, :].astype(F32)
        v = v * lax.rsqrt(jnp.mean(v * v, axis=-1, keepdims=True) + 1e-05)
        v = v.astype(BF)
        dst = pl.ds(al(256 * u + 32 * i, 32), 32)
        for d in range(16):
            lanes = 256 * (2 * (d // 8) + d % 2)
            x[(d // 2) % 4, dst, lanes:lanes + 256] = v[:, 256 * d:256 * d + 256]
        return carry

    lax.fori_loop(0, 8, norm, 0)

    def xcopy(k, q):
        v, dev = [(u, YP), (u, SIB), (u_y, SIB)][k]
        ref = x.at[q, r256(v)]
        return rcopy(ref, ref, xs.at[k, q], xr.at[k, q], dev)

    def xgot(k, q):
        v = [u_y, u_sib, u_yx][k]
        got(x.at[q, r256(v)], xs.at[k, q], xr.at[k, q])

    for q in range(4):
        xcopy(0, q).start()
        xcopy(1, q).start()

    def x_forward(q):
        xgot(0, q)
        xcopy(2, q).start()

    acck[...] = jnp.zeros_like(acck)
    accq[...] = jnp.zeros_like(accq)

    def gemm(yr, lo, hi):
        rows = pl.ds(al(512 * yr, 512), 512)

        def step(q, carry):
            xv = x[q, rows, :]
            acck[rows, :] += jnp.dot(xv, wkvb[q], preferred_element_type=F32)
            for k in (0, 1):
                accq[k, rows, :] += jnp.dot(xv, wqb[k, q], preferred_element_type=F32)
            return carry

        lax.fori_loop(lo, hi, step, 0)

    for ci in (KV, QA, QB):
        fill_wait(ci)
        ring_a(ci)
    for o in range(8):
        hid_remote(o).start()
        hid_local(o).start()
    def keyvals_out(yr):
        kvb[z, yr, 0:512, :] = acck[pl.ds(al(512 * yr, 512), 512), :].astype(BF)

    def queries_out(yr):
        rows = pl.ds(al(512 * yr, 512), 512)
        for p in range(4):
            qs[p, rows, :] = accq[p // 2, rows, 128 * (p % 2):128 * (p % 2) + 128].astype(BF)

    ring_b(KV)
    x_forward(0)
    ring_b(QA)
    for q in range(4):
        xgot(1, q)
    x_forward(1)
    ring_b(QB)
    o_az(0)
    ring_c(KV)
    ring_c(QA)
    ring_c(QB)
    gemm(yh, 0, 4)
    keyvals_out(yh)
    for v in (u_sib, u_y, u_yx):
        got(sgr.at[v], gs.at[0], gr.at[v])
    for k in range(4):
        kvb[z, yh, 512 + 32 * k:544 + 32 * k, :] = sgr[k]
    ring_a(KA)
    x_forward(2)
    ring_b(KA)
    queries_out(yh)
    xgot(2, 0)
    xgot(2, 1)
    gemm(oy, 0, 2)
    xgot(2, 2)
    gemm(oy, 2, 3)
    ring_c(KA)
    o_b1(0)

    below1 = jnp.zeros((16, 128), F32)
    below2 = jnp.zeros((16, 128), F32)
    for q in range(4):
        for t in range(512, 640, 16):
            g = kvb[q, yh, t:t + 16, :].astype(F32)
            below1 = below1 + jnp.where(g < 0.5, 1.0, 0.0)
            below2 = below2 + jnp.where(g < 1.5, 1.0, 0.0)
    n1 = jnp.sum(below1[0:8], axis=-1, keepdims=True)[0:1, :]
    n2 = jnp.sum(below2[0:8], axis=-1, keepdims=True)[0:1, :]
    for r in range(4):
        g = jnp.concatenate(
            [jnp.transpose(jnp.broadcast_to(sgr[r, 16 * k:16 * k + 16, :].astype(F32)[0:1, :], (128, 128)))
             for k in (0, 1)], axis=0)
        start = jnp.where(g < 0.5, 0.0, jnp.where(g < 1.5, n1, n2)).astype(jnp.int32)
        pos = 2048 * (r // 2) + 512 * z + 256 * (r % 2) + row
        lod[r] = jnp.maximum(start, pos - 2047) - lane

    x_forward(3)
    o_ay(0)
    xgot(2, 3)
    last = pl.ds(al(512 * oy, 512), 512)
    acck[last, :] += jnp.dot(x[3, last, :], wkvb[3], preferred_element_type=F32)
    keyvals_out(oy)
    ring_a(KB)
    for k in (0, 1):
        accq[k, last, :] += jnp.dot(x[3, last, :], wqb[k, 3], preferred_element_type=F32)
    queries_out(oy)
    ring_b(KB)
    o_az(1)
    ring_c(KB)

    def attend(yr, cr, mine):
        r = 2 * yr + cr
        rblk = 2 * (4 * yr + z) + cr

        def one(p, carry):
            q2 = qs[p, r256(r), :].astype(F32)
            zero = jnp.zeros_like(q2)
            d1 = lod[r]
            for hh in (0, 1):
                q1 = jnp.where(low, q2 if hh == 0 else pltpu.roll(q2, 64, 1), zero).astype(BF)
                ss = []
                m = jnp.full((256, 128), -1e30, F32)
                for t in range(9):
                    kb = (rblk + t + 8) % 16
                    kk = kvb[(kb // 2) % 4, kb // 8, r256(kb % 2), :]
                    s = lax.dot_general(q1, kk, (((1,), (1,)), ((), ())),
                                        preferred_element_type=F32)
                    base = 256 * (rblk + t) - 2048
                    for v in (0, 1):
                        ok = d1 <= base + 128 * v
                        if t == 8:
                            ok = ok & (row - lane >= 128 * v)
                        su = jnp.where(ok, s[:, 128 * v:128 * v + 128], -1e30)
                        ss.append(su)
                        m = jnp.maximum(m, su)
                mm = jnp.max(m, axis=-1, keepdims=True)
                l = jnp.zeros((256, 128), F32)
                o_ = jnp.zeros((256, 128), F32)
                for t in range(9):
                    kb = (rblk + t + 8) % 16
                    kk = kvb[(kb // 2) % 4, kb // 8, r256(kb % 2), :]
                    w0 = jnp.exp2((ss[2 * t] - mm) * EXP_SCALE)
                    w1 = jnp.exp2((ss[2 * t + 1] - mm) * EXP_SCALE)
                    l = l + w0 + w1
                    o_ = o_ + jnp.dot(jnp.concatenate([w0, w1], axis=1).astype(BF), kk,
                                      preferred_element_type=F32)
                ostat[hh] = o_ / jnp.sum(l, axis=-1, keepdims=True)
            res = jnp.where(low, pltpu.roll(ostat[0], 64, 1), ostat[1]).astype(BF)
            if mine:
                att[r256(cr), pl.ds(al(512 * u + 128 * p, 128), 128)] = res
            else:
                atx[cr, :, pl.ds(al(128 * p, 128), 128)] = res
            return carry

        lax.fori_loop(0, 4, one, 0, unroll=2)

    def ablk(cr, v):
        return att.at[r256(cr), pl.ds(al(512 * v, 512), 512)]

    def acopy(k, cr):
        src, dst, dev = [
            lambda: (atx.at[cr], ablk(cr, u), YP),
            lambda: (ablk(cr, u), ablk(cr, u), SIB),
            lambda: (ablk(cr, u_y), ablk(cr, u_y), SIB),
        ][k]()
        return rcopy(src, dst, axs.at[k, cr], axr.at[k, cr], dev)

    def agot(k, cr):
        got(ablk(cr, [u_y, u_sib, u_yx][k]), axs.at[k, cr], axr.at[k, cr])

    def out_cols(o, cc, h):
        return out.at[:, pl.ds(al(256 * (2 * o + cc) + 128 * h, 128), 128)]

    def pass_copy(h, o, cr):
        return rcopy(outb.at[h, o, cr], out_cols(o, c, h), ps.at[h, o, cr], pr.at[h, o, c], NX[cr])

    def project(cr, h, n, dy, dz):
        def step(i, carry):
            o = own(dy(i), dz(i))
            v = jnp.dot(att[r256(cr), :], wob[h, o], preferred_element_type=F32)
            r = v + hf[cr, o, :, 128 * h:128 * h + 128].astype(F32)
            outb[h, o, cr] = r.astype(BF)
            pass_copy(h, o, cr).start()
            return carry

        lax.fori_loop(0, n, step, 0)

    def project_b(cr, h):
        project(cr, h, 3, lambda i: 0, lambda i: i + i // 2)
        project(cr, h, 1, lambda i: 1, lambda i: 0)

    def project_z(cr, h):
        project(cr, h, 1, lambda i: 0, lambda i: 2)

    def project_c(cr, h):
        project(cr, h, 2, lambda i: 1, lambda i: 1 + 2 * i)

    def project_d(cr, h):
        project(cr, h, 1, lambda i: 1, lambda i: 2)

    attend(oy, 0, False)
    acopy(0, 0).start()
    o_ay(1)
    o_b2(0)
    attend(oy, 1, False)
    acopy(0, 1).start()
    o_b1(1)
    agot(0, 0)
    acopy(2, 0).start()
    for o in range(8):
        hid_local(o).wait()
        got(hf.at[oc, o], hs.at[o], hr.at[o])
    attend(yh, 0, True)
    acopy(1, 0).start()
    agot(0, 1)
    acopy(2, 1).start()
    o_zz(0)
    agot(1, 0)
    agot(2, 0)
    project_b(0, 0)
    o_c(0)
    o_b2(1)
    project_z(0, 0)
    project_c(0, 0)
    project_b(0, 1)
    attend(yh, 1, True)
    acopy(1, 1).start()
    o_zz(1)
    project_z(0, 1)
    agot(1, 1)
    agot(2, 1)
    project_b(1, 0)
    project_z(1, 0)
    project_c(1, 0)
    project_b(1, 1)
    project_z(1, 1)
    o_c(1)
    o_d(0)
    project_d(0, 0)
    project_d(1, 0)
    project_c(0, 1)
    project_c(1, 1)
    o_d(1)
    project_d(0, 1)
    project_d(1, 1)

    for ci in range(5):
        for i in range(4):
            ring(ci, i).wait_send()
        if ci < KA:
            for n in range(3):
                fill(ci, n).wait_send()
    for h in (0, 1):
        for i in range(9):
            osend(h, i).wait_send()
    for n in range(3):
        segs(n).wait_send()
    for k in range(3):
        for q in range(4):
            xcopy(k, q).wait_send()
        for cr in (0, 1):
            acopy(k, cr).wait_send()
    for o in range(8):
        hid_remote(o).wait_send()
    for h in (0, 1):
        for o in range(8):
            for cc in (0, 1):
                pass_copy(h, o, cc).wait_send()
                got(out_cols(o, cc, h), ps.at[h, o, cc], pr.at[h, o, cc])


def body(section_input, segment_ids, query_weight, keyval_weight, out_weight):
    vm = pl.BlockSpec(memory_space=pltpu.VMEM)
    hb = pl.BlockSpec(memory_space=pl.ANY)
    dma = pltpu.SemaphoreType.DMA
    res = pl.pallas_call(
        kernel,
        out_shape=jax.ShapeDtypeStruct((256, 4096), BF),
        in_specs=[vm, vm, hb, vm, hb],
        out_specs=hb,
        scratch_shapes=[
            pltpu.VMEM((4, 1024, 1024), BF),
            pltpu.VMEM((2, 4, 1024, 256), BF),
            pltpu.VMEM((4, 1024, 128), BF),
            pltpu.VMEM((2, 8, 2048, 128), BF),
            pltpu.VMEM((4, 2, 640, 128), BF),
            pltpu.VMEM((4, 1024, 128), BF),
            pltpu.VMEM((512, 2048), BF),
            pltpu.VMEM((2, 256, 512), BF),
            pltpu.VMEM((2, 8, 256, 256), BF),
            pltpu.VMEM((2, 8, 2, 256, 128), BF),
            pltpu.VMEM((2, 1024, 256), F32),
            pltpu.VMEM((1024, 128), F32),
            pltpu.VMEM((2, 256, 128), F32),
            pltpu.VMEM((4, 32, 128), BF),
            pltpu.VMEM((4, 256, 128), jnp.int32),
            pltpu.VMEM((4, 256, 128), BF),
            dma((3, 3)), dma((3, 4)), dma((3,)),
            dma((5, 4)), dma((5, 4)),
            dma((2, 9)), dma((2, 9)), dma((2,)),
            dma((3, 4)), dma((3, 4)),
            dma((8,)), dma((8,)), dma((8,)),
            dma((3,)), dma((4,)),
            dma((3, 2)), dma((3, 2)),
            dma((2, 8, 2)), dma((2, 8, 2)),
        ],
        compiler_params=pltpu.CompilerParams(
            collective_id=0, has_side_effects=True, vmem_limit_bytes=58 << 20),
        name="layer",
    )(section_input[0], segment_ids, query_weight[0], keyval_weight[0], out_weight[0])
    return res[None]


def solution(mesh):
    fine = Mesh(mesh.devices.reshape(8, 2, 4, 2), ("section", "yh", "z", "core"))
    tok = ("yh", "z", "core")
    return jax.shard_map(
        body,
        mesh=fine,
        in_specs=(
            P("section", tok, None),
            P("section", tok),
            P("section", tok, None),
            P("section", tok, None),
            P("section", None, tok),
        ),
        out_specs=P("section", tok, None),
        check_vma=False,
    )
```
